32 devices in a mesh: gx: 4 (over z), gy: 8 (over y, x, core).
Axes of the slice: x: 2, y: 2, z: 4, core: 2. Of those that a mesh axis runs over, the one named last changes fastest.
Arguments:
- operator_blocks: bfloat16 [256, 6, 256, 256], P(('gx', 'gy')), may hold values from -0.15625 to 0.15625
- local_columns: int32 [256, 2], P(('gx', 'gy')), may hold values from 0 to 7
- remote_columns: int32 [256, 4], P(('gx', 'gy')), may hold values from 8 to 17
- match_slots: int32 [256, 6, 2], P(('gx', 'gy')), may hold values from 0 to 2
- tentative: bfloat16 [256, 2, 256, 256], P(('gx', 'gy')), may hold values from -1.5 to 1.5
- inverse_diagonal: bfloat16 [256, 256, 256], P(('gx', 'gy')), may hold values from -0.375 to 0.375
- peer_sends: int32 [32, 8], P(('gx', 'gy')), may hold values from 0 to 7
- slab_sends: int32 [32, 2], P(('gx', 'gy')), may hold values from 0 to 7
- coarse_slots: int32 [256, 2, 2], P(('gx', 'gy')), may hold values from 0 to 47, as said below
Outputs:
- smoothed: bfloat16 [256, 2, 256, 256], P(('gx', 'gy'))
- coarse_operator: bfloat16 [192, 256, 256], P(('gx', 'gy'))
The draws below stay inside these ranges and needn't reach their ends.
Inputs may be any that keep to these rules, and one draw needn't show every extreme that they name: `match_slots`: the value 2 stands for no matching block. `coarse_slots`: no two partial blocks of one device name the same coarse block; coarse block c of a slab belongs to the device of gy index c // 6.
All inputs are finite; a program needn't handle non-finite values.
Results may differ from the reference program's by a relative error of at most 0.012.
Values may be sent and summed in bfloat16 or wider, within the bound.
A program may use at most 128 MiB of HBM per device.

```python
import jax
import jax.numpy as jnp
from jax import lax

B = 256
R = 8
KL = 2
KO = 4
K = 6
KP = 2
S = 1
H = 1
NB = 256
NEXT = 18
CS = 6
NCOARSE = 192
N_GX = 4
N_GY = 8


def draw_coarse_slots(key, part):
    devices = N_GX * N_GY
    total = N_GY * CS
    per_device = R * KP * KP
    key_bias, key_hot, key_noise, key_order = jax.random.split(key, 4)
    bias = jax.random.randint(key_bias, (N_GX, N_GY), 0, 4)
    hot = jax.random.randint(key_hot, (N_GX,), 0, N_GY)
    bias = jnp.where(jnp.arange(N_GY)[None, :] == hot[:, None], 4, bias)
    slot_ids = jnp.arange(total, dtype=jnp.int32)
    owner = slot_ids // CS
    slab = jnp.arange(devices, dtype=jnp.int32) // N_GY
    weight = bias[slab][:, owner]
    weight = jnp.where(((slot_ids == 0) | (slot_ids == total - 1))[None, :], 5, weight)
    noise = jax.random.randint(key_noise, (devices, total), 0, 65536)
    scores = (weight * 65536 + noise) * total + slot_ids[None, :]
    _, picked = lax.top_k(scores, per_device)
    order_keys = jax.random.randint(key_order, (devices, per_device), 0, 65536) * per_device + jnp.arange(per_device, dtype=jnp.int32)[None, :]
    order = jnp.argsort(order_keys, axis=1, stable=True)
    shuffled = jnp.take_along_axis(picked, order, axis=1)
    return shuffled.astype(jnp.int32).reshape(NB, KP, KP)


def touch_ends(values, stream_key, smallest, largest):
    index_at = [jax.random.randint(jax.random.fold_in(stream_key, axis), (), 0, length) for axis, length in enumerate(values.shape)]
    longest = values.shape.index(max(values.shape))
    neighbour = index_at[:longest] + [(index_at[longest] + 1) % values.shape[longest]] + index_at[longest + 1:]
    return values.at[tuple(index_at)].set(smallest).at[tuple(neighbour)].set(largest)


def levels(own_key, extent, cuts, smallest, high):
    def one(axis_at, blocks):
        heights = jax.random.uniform(jax.random.fold_in(jax.random.fold_in(own_key, 6), axis_at), (blocks,), jnp.float32, smallest / len(cuts), high / len(cuts))
        return jnp.repeat(jnp.exp(heights), extent[axis_at] // blocks).reshape((-1,) + (1,) * (len(extent) - axis_at - 1))

    factor_of = one(*cuts[0])
    for cut in cuts[1:]:
        factor_of = factor_of * one(*cut)
    return factor_of


def gaussian(own_key, shape, scale, bound, cuts=(), kind=jnp.bfloat16):
    factor_of = levels(own_key, shape, cuts, -0.22, 0.18) if cuts else 1.0
    array = jax.random.normal(own_key, shape, jnp.float32) * scale * factor_of
    return jnp.minimum(jnp.maximum(array, -bound), bound).astype(kind)


def setup_inputs(seed: int = 0) -> dict:
    key_of = jax.random.split(jax.random.key(seed), 10)
    return {
        "operator_blocks": gaussian(key_of[0], (NB, K, B, B), (K * B) ** -0.5, 0.15625, ((0, 32),)),
        "local_columns": touch_ends(jax.random.randint(key_of[1], (NB, KL), 0, R), jax.random.fold_in(key_of[1], 1), 0, R - 1).astype(jnp.int32),
        "remote_columns": touch_ends(jax.random.randint(key_of[2], (NB, KO), R, NEXT), jax.random.fold_in(key_of[2], 1), R, NEXT - 1).astype(jnp.int32),
        "match_slots": touch_ends(jax.random.randint(key_of[3], (NB, K, KP), 0, KP + 1), jax.random.fold_in(key_of[3], 1), 0, KP).astype(jnp.int32),
        "tentative": gaussian(key_of[4], (NB, KP, B, B), 0.25, 1.5, ((0, 32),)),
        "inverse_diagonal": gaussian(key_of[5], (NB, B, B), B ** -0.5, 0.375, ((0, 32),)),
        "peer_sends": touch_ends(jax.random.randint(key_of[6], (N_GX * N_GY, N_GY * S), 0, R), jax.random.fold_in(key_of[6], 1), 0, R - 1).astype(jnp.int32),
        "slab_sends": touch_ends(jax.random.randint(key_of[7], (N_GX * N_GY, 2 * H), 0, R), jax.random.fold_in(key_of[7], 1), 0, R - 1).astype(jnp.int32),
        "coarse_slots": draw_coarse_slots(jax.random.fold_in(key_of[9], 71), 0),
    }


def select_blocks(picked, matches):
    selected = []
    for out_block in range(matches.shape[2]):
        chosen = jnp.zeros_like(picked[:, :, 0])
        for in_block in range(picked.shape[2]):
            matched = (matches[:, :, out_block] == in_block)[:, :, None, None]
            chosen = jnp.where(matched, picked[:, :, in_block], chosen)
        selected.append(chosen)
    return jnp.stack(selected, axis=2)


def table_map(peer_sends, slab_sends):
    devices = N_GX * N_GY
    device = jnp.arange(devices, dtype=jnp.int32)
    slab = device // N_GY
    member = device % N_GY
    own_rows = device[:, None] * R + jnp.arange(R, dtype=jnp.int32)[None, :]
    entry = jnp.arange(N_GY * S, dtype=jnp.int32)
    source = slab[:, None] * N_GY + entry[None, :] // S
    position = member[:, None] * S + entry[None, :] % S
    peer_rows = source * R + peer_sends[source, position]
    below = jnp.clip(device - N_GY, 0, devices - 1)
    above = jnp.clip(device + N_GY, 0, devices - 1)
    lower_rows = jnp.where((slab >= 1)[:, None], below[:, None] * R + slab_sends[below, :H], NB)
    upper_rows = jnp.where((slab < N_GX - 1)[:, None], above[:, None] * R + slab_sends[above, H:], NB)
    return jnp.concatenate([own_rows, peer_rows, lower_rows, upper_rows], axis=1).astype(jnp.int32)


def product_rows(padded, blocks, columns, matches):
    picked = padded[columns].astype(jnp.float32)
    chosen = select_blocks(picked, matches)
    return jnp.einsum('rkab,rknbc->rnac', blocks.astype(jnp.float32), chosen, precision=lax.Precision.HIGHEST)


def reference(operator_blocks, local_columns, remote_columns, match_slots, tentative, inverse_diagonal, peer_sends, slab_sends, coarse_slots):
    devices = N_GX * N_GY
    lookup = table_map(peer_sends, slab_sends)
    columns = jnp.concatenate([local_columns, remote_columns], axis=1).astype(jnp.int32)
    owner_device = (jnp.arange(NB, dtype=jnp.int32) // R)[:, None]
    global_columns = lookup[owner_device, columns].astype(jnp.int32)
    blocks_dev = operator_blocks.reshape(devices, R, K, B, B)
    columns_dev = global_columns.reshape(devices, R, K)
    matches_dev = match_slots.reshape(devices, R, K, KP)
    inverse_dev = inverse_diagonal.reshape(devices, R, B, B)
    fine_rows = tentative
    for smooth_pass in range(2):
        padded = jnp.concatenate([fine_rows, jnp.zeros((1, KP, B, B), fine_rows.dtype)], axis=0)

        def smooth_device(inputs):
            blocks, device_columns, matches, inverse, rows = inputs
            image = lax.optimization_barrier(product_rows(padded, blocks, device_columns, matches).astype(jnp.bfloat16))
            update = jnp.einsum('rab,rnbc->rnac', inverse.astype(jnp.float32), image.astype(jnp.float32), precision=lax.Precision.HIGHEST)
            return (rows.astype(jnp.float32) - update).astype(jnp.bfloat16)

        fine_rows = lax.map(smooth_device, (blocks_dev, columns_dev, matches_dev, inverse_dev, fine_rows.reshape(devices, R, KP, B, B))).reshape(NB, KP, B, B)
    padded = jnp.concatenate([fine_rows, jnp.zeros((1, KP, B, B), fine_rows.dtype)], axis=0)
    slots_dev = coarse_slots.reshape(devices, R * KP * KP)

    def accumulate(total, inputs):
        blocks, device_columns, matches, rows, slots, device = inputs
        image = lax.optimization_barrier(product_rows(padded, blocks, device_columns, matches).astype(jnp.bfloat16))
        partial_value = jnp.einsum('rnab,rmac->rnmbc', rows.astype(jnp.float32), image.astype(jnp.float32), precision=lax.Precision.HIGHEST)
        partial_value = lax.optimization_barrier(partial_value.astype(jnp.bfloat16)).astype(jnp.float32).reshape(R * KP * KP, B, B)
        targets = (device // N_GY) * (N_GY * CS) + slots
        return total.at[targets].add(partial_value), None

    start = jnp.zeros((NCOARSE, B, B), jnp.float32)
    total, _ = lax.scan(accumulate, start, (blocks_dev, columns_dev, matches_dev, fine_rows.reshape(devices, R, KP, B, B), slots_dev, jnp.arange(devices, dtype=jnp.int32)))
    return fine_rows, total.astype(jnp.bfloat16)
```

```python
import functools

import jax
import jax.numpy as jnp
from jax import lax
from jax.experimental import pallas as pl
from jax.experimental.pallas import tpu as pltpu
from jax.sharding import PartitionSpec as P

MESH = pl.DeviceIdType.MESH
STRIPES = 2


def side_by_side(parts):
    return parts[0] if len(parts) == 1 else jnp.concatenate(parts, axis=1)


def kernel(
    dims,
    local_ref,
    remote_ref,
    match_ref,
    peer_ref,
    slab_ref,
    slots_ref,
    operator_hbm,
    tentative_hbm,
    diagonal_hbm,
    smooth_hbm,
    coarse_ref,
    operator,
    diagonal,
    send,
    local_sum,
    turned,
    partial,
    outgoing,
    total,
    table,
    inverse,
    *rest,
):
    slabs, group, rows, kl, ko, kp, peers, halo, owned = dims
    bits = group.bit_length() - 1
    owns, rest = rest[:STRIPES], rest[STRIPES:]
    rems, rest = (rest[:STRIPES], rest[STRIPES : 2 * STRIPES]), rest[2 * STRIPES :]
    landed = rest[:bits]
    (
        load_sem,
        rows_sem,
        out_sem,
        send_sem,
        recv_sem,
        slab_send_sem,
        slab_recv_sem,
        half_send_sem,
        half_recv_sem,
    ) = rest[bits:]
    width = operator.shape[-1]
    columns = width // STRIPES
    gx = lax.axis_index("gx")
    me = lax.axis_index("gy")
    has_below = gx > 0
    has_above = gx < slabs - 1
    own_zero = rows * kp
    rem_zero = (group * peers + 2 * halo) * kp
    count = rows * kp * kp
    span = peers * kp
    slab_span = halo * kp
    slab_at = group * span

    def load_rows(s):
        return pltpu.make_async_copy(
            tentative_hbm.at[:, :, pl.ds(s * columns, columns)],
            owns[s].at[pl.ds(0, own_zero)],
            rows_sem.at[s],
        )

    for s in range(STRIPES):
        load_rows(s).start()
    load_operator = pltpu.make_async_copy(operator_hbm, operator, load_sem.at[0])
    load_operator.start()
    load_diagonal = pltpu.make_async_copy(diagonal_hbm, diagonal, load_sem.at[1])
    load_diagonal.start()

    barrier = pltpu.get_barrier_semaphore()

    def greet(offset, carry):
        pl.semaphore_signal(
            barrier, inc=1, device_id=(gx, (me + offset) % group), device_id_type=MESH
        )
        return carry

    lax.fori_loop(1, group, greet, 0)

    @pl.when(has_below)
    def _():
        pl.semaphore_signal(barrier, inc=1, device_id=(gx - 1, me), device_id_type=MESH)

    @pl.when(has_above)
    def _():
        pl.semaphore_signal(barrier, inc=1, device_id=(gx + 1, me), device_id_type=MESH)

    zero = jnp.zeros((width, columns), jnp.bfloat16)
    for s in range(STRIPES):
        owns[s][own_zero] = zero
        for rem in rems:
            rem[s][rem_zero] = zero
        partial[s, count] = zero
    neighbours = jnp.where(has_below, 1, 0) + jnp.where(has_above, 1, 0)
    pl.semaphore_wait(barrier, group - 1 + neighbours)

    def peer_copy(step, s, offset):
        return pltpu.make_async_remote_copy(
            src_ref=send.at[s, pl.ds(offset * span, span)],
            dst_ref=rems[step % 2][s].at[pl.ds(me * span, span)],
            send_sem=send_sem.at[step, s, offset],
            recv_sem=recv_sem.at[step, s, offset],
            device_id=(gx, (me + offset) % group),
            device_id_type=MESH,
        )

    def slab_copy(step, s, way):
        at = slab_at + way * slab_span
        return pltpu.make_async_remote_copy(
            src_ref=send.at[s, pl.ds(at, slab_span)],
            dst_ref=rems[step % 2][s].at[pl.ds(at, slab_span)],
            send_sem=slab_send_sem.at[step, s, way],
            recv_sem=slab_recv_sem.at[step, s, way],
            device_id=(gx + 1 - 2 * way, me),
            device_id_type=MESH,
        )

    def post_rows(step, s):
        def post(turn, carry):
            offset = 1 + (2 * turn + 1) % (group - 1)
            target = (me + offset) % group
            for p in range(peers):
                row = peer_ref[0, target * peers + p]
                for n in range(kp):
                    send[s, offset * span + p * kp + n] = owns[s][row * kp + n]
            peer_copy(step, s, offset).start()
            return carry

        lax.fori_loop(0, group - 1, post, 0)
        for way, present in enumerate((has_above, has_below)):

            @pl.when(present)
            def _():
                for h in range(halo):
                    row = slab_ref[0, way * halo + h]
                    for n in range(kp):
                        send[s, slab_at + way * slab_span + h * kp + n] = owns[s][row * kp + n]
                slab_copy(step, s, way).start()

        for p in range(peers):
            row = peer_ref[0, me * peers + p]
            for n in range(kp):
                rems[step % 2][s][me * span + p * kp + n] = owns[s][row * kp + n]

    def arrive(step, s):
        def finish(turn, carry):
            peer_copy(step, s, 1 + (2 * turn + 1) % (group - 1)).wait()
            return carry

        lax.fori_loop(0, group - 1, finish, 0)
        for way, (sends, receives) in enumerate(((has_above, has_below), (has_below, has_above))):

            @pl.when(sends)
            def _():
                slab_copy(step, s, way).wait_send()

            @pl.when(receives)
            def _():
                slab_copy(step, s, way).wait_recv()

    def tabulate(row, carry):
        for k in range(kl):
            for n in range(kp):
                match = match_ref[k, n, row]
                table[k, n, row] = jnp.where(
                    match == kp, own_zero, local_ref[k, row] * kp + match
                )
        for k in range(ko):
            source = jnp.maximum(remote_ref[k, row] - rows, 0)
            from_below = (source >= group * peers) & (source < group * peers + halo)
            from_above = source >= group * peers + halo
            missing = (from_below & (gx == 0)) | (from_above & (gx == slabs - 1))
            for n in range(kp):
                match = match_ref[kl + k, n, row]
                table[kl + k, n, row] = jnp.where(
                    (match == kp) | missing, rem_zero, source * kp + match
                )
        return carry

    def product(row, first, last, rows_of):
        blocks = [operator[row, k] for k in range(first, last)]
        picked = [
            side_by_side([rows_of[table[k, n, row]] for n in range(kp)])
            for k in range(first, last)
        ]
        return jnp.dot(
            jnp.concatenate(blocks, axis=1),
            jnp.concatenate(picked, axis=0),
            preferred_element_type=jnp.float32,
        )

    def local_rows(s):
        def local_row(row, carry):
            local_sum[s, row] = product(row, 0, kl, owns[s])
            return carry

        lax.fori_loop(0, rows, local_row, 0)

    def image_of(row, step, s):
        value = local_sum[s, row] + product(row, kl, kl + ko, rems[step % 2][s])
        return value.astype(jnp.bfloat16)

    def smooth_rows(step, s):
        def smooth_row(row, carry):
            update = jnp.dot(
                diagonal[row], image_of(row, step, s), preferred_element_type=jnp.float32
            )
            for n in range(kp):
                before = owns[s][row * kp + n].astype(jnp.float32)
                after = before - update[:, n * columns : (n + 1) * columns]
                owns[s][row * kp + n] = after.astype(jnp.bfloat16)
            return carry

        lax.fori_loop(0, rows, smooth_row, 0)

    def turn_row(row, carry):
        for n in range(kp):
            for s in range(STRIPES):
                turned[row * kp + n, pl.ds(s * columns, columns)] = owns[s][row * kp + n].T
        return carry

    def partial_rows(step, s):
        def partial_row(row, carry):
            image = image_of(row, step, s)
            for n in range(kp):
                blocks = jnp.dot(
                    turned[row * kp + n], image, preferred_element_type=jnp.float32
                ).astype(jnp.bfloat16)
                for m in range(kp):
                    at = (row * kp + n) * kp + m
                    partial[s, at] = blocks[:, m * columns : (m + 1) * columns]
            return carry

        lax.fori_loop(0, rows, partial_row, 0)

    core = me % 2
    half = group * owned // 2
    grain = owned // 2 if owned % 2 == 0 else owned

    def invert(at, carry):
        place = at // owned
        high = place // (group // 2)
        odd = (high + me) % 2
        other = high
        for step in range(1, bits):
            bit = (place >> (bits - 1 - step)) & 1
            other = other | jnp.where(odd == 0, bit << step, bit << (bits - step))
        slot = (me ^ other) * owned + at % owned
        found = count
        for row in range(rows):
            for n in range(kp):
                for m in range(kp):
                    named = (row * kp + n) * kp + m
                    found = jnp.where(slots_ref[n, m, row] == slot, named, found)
        inverse[at] = found
        return carry

    def partner(step):
        def flip(bit):
            return me + bit * (1 - 2 * ((me // bit) % 2))

        if step == 0:
            return flip(1)
        return (1 - core) * flip(1 << step) + core * flip(1 << (bits - step))

    def half_copy(step, s, chunk):
        at = chunk * grain
        if step == 0:
            source = outgoing.at[s, pl.ds(at, grain)]
        else:
            source = total.at[s, pl.ds((half >> step) + at, grain)]
        return pltpu.make_async_remote_copy(
            src_ref=source,
            dst_ref=landed[step].at[s, pl.ds(at, grain)],
            send_sem=half_send_sem.at[step, s, chunk],
            recv_sem=half_recv_sem.at[step, s, chunk],
            device_id=(gx, partner(step)),
            device_id_type=MESH,
        )

    def send_partials(s):
        def send_chunk(turn, carry):
            chunk = half // grain - 1 - turn
            for j in range(grain):
                at = chunk * grain + j
                outgoing[s, at] = partial[s, inverse[half + at]]
            half_copy(0, s, chunk).start()
            return carry

        lax.fori_loop(0, half // grain, send_chunk, 0)

    def add_partials(step, s):
        last = step == bits - 1
        chunks = (half >> step) // grain

        def add(chunk):
            half_copy(step, s, chunk).wait_recv()
            for j in range(grain):
                at = chunk * grain + j
                mine = partial[s, inverse[at]] if step == 0 else total[s, at]
                value = mine.astype(jnp.float32) + landed[step][s, at].astype(jnp.float32)
                if last:
                    coarse_ref[at, :, s * columns : (s + 1) * columns] = value.astype(jnp.bfloat16)
                else:
                    total[s, at] = value.astype(jnp.bfloat16)

        if last:
            for chunk in reversed(range(chunks)):
                add(chunk)
            return

        def upper(turn, carry):
            chunk = chunks - 1 - turn
            add(chunk)
            half_copy(step + 1, s, chunk - chunks // 2).start()
            return carry

        def lower(turn, carry):
            add(chunks // 2 - 1 - turn)
            return carry

        lax.fori_loop(0, chunks // 2, upper, 0)
        lax.fori_loop(0, chunks // 2, lower, 0)

    stripes = range(STRIPES)
    load_rows(0).wait()
    post_rows(0, 0)
    lax.fori_loop(0, rows, tabulate, 0)
    for s in stripes[1:]:
        load_rows(s).wait()
    load_operator.wait()
    for s in stripes:
        local_rows(s)
    for s in stripes[1:]:
        post_rows(0, s)
    lax.fori_loop(0, group * owned, invert, 0)
    load_diagonal.wait()

    stores = []
    for step in range(2):
        for s in stripes:
            arrive(step, s)
            smooth_rows(step, s)
            post_rows(step + 1, s)
            if step == 1:
                store = pltpu.make_async_copy(
                    owns[s].at[pl.ds(0, own_zero)],
                    smooth_hbm.at[:, :, pl.ds(s * columns, columns)],
                    out_sem.at[s],
                )
                store.start()
                stores.append(store)
            local_rows(s)
    lax.fori_loop(0, rows, turn_row, 0)

    for s in stripes:
        if s > 0:
            add_partials(0, s - 1)
        arrive(2, s)
        partial_rows(2, s)
        send_partials(s)
    for step in range(1, bits):
        add_partials(step, 0)
        add_partials(step - 1, 1)
    add_partials(bits - 1, 1)
    for s in stripes:
        for step in range(bits):
            for chunk in range((half >> step) // grain):
                half_copy(step, s, chunk).wait_send()
    for store in stores:
        store.wait()


def body(
    operator_blocks,
    local_columns,
    remote_columns,
    match_slots,
    tentative,
    inverse_diagonal,
    peer_sends,
    slab_sends,
    coarse_slots,
):
    slabs = lax.axis_size("gx")
    group = lax.axis_size("gy")
    rows, kp, width = tentative.shape[:3]
    kl, ko = local_columns.shape[1], remote_columns.shape[1]
    peers = peer_sends.shape[1] // group
    halo = slab_sends.shape[1] // 2
    owned = (3 * rows * kp * kp // 2 + group - 1) // group
    bits = group.bit_length() - 1
    count = rows * kp * kp
    columns = width // STRIPES
    dims = (slabs, group, rows, kl, ko, kp, peers, halo, owned)

    def blocks(n):
        return pltpu.VMEM((STRIPES, n, width, columns), jnp.bfloat16)

    smem = pl.BlockSpec(memory_space=pltpu.SMEM)
    anywhere = pl.BlockSpec(memory_space=pl.ANY)
    half = group * owned // 2
    remote_count = (group * peers + 2 * halo) * kp
    smoothed, coarse = pl.pallas_call(
        functools.partial(kernel, dims),
        out_shape=(
            jax.ShapeDtypeStruct((rows * kp, width, width), jnp.bfloat16),
            jax.ShapeDtypeStruct((owned, width, width), jnp.bfloat16),
        ),
        in_specs=[smem] * 6 + [anywhere] * 3,
        out_specs=(anywhere, pl.BlockSpec(memory_space=pltpu.VMEM)),
        scratch_shapes=[
            pltpu.VMEM(operator_blocks.shape, jnp.bfloat16),
            pltpu.VMEM((rows, width, width), jnp.bfloat16),
            blocks(remote_count),
            pltpu.VMEM((STRIPES, rows, width, kp * columns), jnp.float32),
            pltpu.VMEM((rows * kp, width, width), jnp.bfloat16),
            blocks(count + 1),
            blocks(half),
            blocks(half),
            pltpu.SMEM((kl + ko, kp, rows), jnp.int32),
            pltpu.SMEM((2 * half,), jnp.int32),
            *[pltpu.VMEM((rows * kp + 1, width, columns), jnp.bfloat16)] * STRIPES,
            *[pltpu.VMEM((remote_count + 1, width, columns), jnp.bfloat16)] * (2 * STRIPES),
            *[blocks(half >> step) for step in range(bits)],
            pltpu.SemaphoreType.DMA((2,)),
            pltpu.SemaphoreType.DMA((STRIPES,)),
            pltpu.SemaphoreType.DMA((STRIPES,)),
            pltpu.SemaphoreType.DMA((3, STRIPES, group)),
            pltpu.SemaphoreType.DMA((3, STRIPES, group)),
            pltpu.SemaphoreType.DMA((3, STRIPES, 2)),
            pltpu.SemaphoreType.DMA((3, STRIPES, 2)),
            pltpu.SemaphoreType.DMA((bits, STRIPES, group)),
            pltpu.SemaphoreType.DMA((bits, STRIPES, group)),
        ],
        compiler_params=pltpu.CompilerParams(
            collective_id=0, has_side_effects=True, vmem_limit_bytes=67_000_000
        ),
    )(
        local_columns.T,
        remote_columns.T,
        match_slots.transpose(1, 2, 0),
        peer_sends,
        slab_sends,
        coarse_slots.transpose(1, 2, 0),
        operator_blocks,
        tentative.reshape(rows * kp, width, width),
        inverse_diagonal,
    )
    return smoothed.reshape(tentative.shape), coarse


def solution(mesh):
    placed = (
        P(("gx", "gy"), None, None, None),
        P(("gx", "gy"), None),
        P(("gx", "gy"), None),
        P(("gx", "gy"), None, None),
        P(("gx", "gy"), None, None, None),
        P(("gx", "gy"), None, None),
        P(("gx", "gy"), None),
        P(("gx", "gy"), None),
        P(("gx", "gy"), None, None),
    )
    return jax.shard_map(
        body,
        mesh=mesh,
        in_specs=placed,
        out_specs=(P(("gx", "gy"), None, None, None), P(("gx", "gy"), None, None)),
        check_vma=False,
    )
```

```python
import functools

import jax
import jax.numpy as jnp
from jax import lax
from jax.experimental import pallas as pl
from jax.experimental.pallas import tpu as pltpu
from jax.sharding import PartitionSpec as P

MESH = pl.DeviceIdType.MESH
STRIPES = 2


def side_by_side(parts):
    return parts[0] if len(parts) == 1 else jnp.concatenate(parts, axis=1)


def kernel(
    dims,
    local_hbm,
    remote_hbm,
    match_hbm,
    peer_hbm,
    slab_hbm,
    slots_hbm,
    operator_hbm,
    tentative_hbm,
    diagonal_hbm,
    smooth_hbm,
    coarse_ref,
    operator,
    diagonal,
    send,
    local_sum,
    turned,
    partial,
    outgoing,
    total,
    local_ref,
    remote_ref,
    match_ref,
    peer_ref,
    slab_ref,
    slots_ref,
    table,
    inverse,
    *rest,
):
    slabs, group, rows, kl, ko, kp, peers, halo, owned = dims
    bits = group.bit_length() - 1
    owns, rest = rest[:STRIPES], rest[STRIPES:]
    rems, rest = (rest[:STRIPES], rest[STRIPES : 2 * STRIPES]), rest[2 * STRIPES :]
    landed = rest[:bits]
    (
        index_sem,
        load_sem,
        rows_sem,
        out_sem,
        send_sem,
        recv_sem,
        slab_send_sem,
        slab_recv_sem,
        half_send_sem,
        half_recv_sem,
    ) = rest[bits:]
    width = operator.shape[-1]
    columns = width // STRIPES
    gx = lax.axis_index("gx")
    me = lax.axis_index("gy")
    has_below = gx > 0
    has_above = gx < slabs - 1
    own_zero = rows * kp
    rem_zero = (group * peers + 2 * halo) * kp
    count = rows * kp * kp
    span = peers * kp
    slab_span = halo * kp
    slab_at = group * span

    def load_rows(s):
        return pltpu.make_async_copy(
            tentative_hbm.at[:, :, pl.ds(s * columns, columns)],
            owns[s].at[pl.ds(0, own_zero)],
            rows_sem.at[s],
        )

    load_peers = pltpu.make_async_copy(peer_hbm, peer_ref, index_sem.at[0])
    load_slabs = pltpu.make_async_copy(slab_hbm, slab_ref, index_sem.at[1])
    load_matches = pltpu.make_async_copy(match_hbm, match_ref, index_sem.at[2])
    load_locals = pltpu.make_async_copy(local_hbm, local_ref, index_sem.at[3])
    load_remotes = pltpu.make_async_copy(remote_hbm, remote_ref, index_sem.at[4])
    load_slots = pltpu.make_async_copy(slots_hbm, slots_ref, index_sem.at[5])
    load_rows(0).start()
    for load in (load_peers, load_slabs, load_matches, load_locals, load_remotes, load_slots):
        load.start()
    for s in range(1, STRIPES):
        load_rows(s).start()
    load_operator = pltpu.make_async_copy(operator_hbm, operator, load_sem.at[0])
    load_operator.start()
    load_diagonal = pltpu.make_async_copy(diagonal_hbm, diagonal, load_sem.at[1])
    load_diagonal.start()

    barrier = pltpu.get_barrier_semaphore()

    def greet(offset, carry):
        pl.semaphore_signal(
            barrier, inc=1, device_id=(gx, (me + offset) % group), device_id_type=MESH
        )
        return carry

    lax.fori_loop(1, group, greet, 0)

    @pl.when(has_below)
    def _():
        pl.semaphore_signal(barrier, inc=1, device_id=(gx - 1, me), device_id_type=MESH)

    @pl.when(has_above)
    def _():
        pl.semaphore_signal(barrier, inc=1, device_id=(gx + 1, me), device_id_type=MESH)

    zero = jnp.zeros((width, columns), jnp.bfloat16)
    for s in range(STRIPES):
        owns[s][own_zero] = zero
        for rem in rems:
            rem[s][rem_zero] = zero
        partial[s, count] = zero
    neighbours = jnp.where(has_below, 1, 0) + jnp.where(has_above, 1, 0)
    pl.semaphore_wait(barrier, group - 1 + neighbours)

    def peer_copy(step, s, offset):
        return pltpu.make_async_remote_copy(
            src_ref=send.at[s, pl.ds(offset * span, span)],
            dst_ref=rems[step % 2][s].at[pl.ds(me * span, span)],
            send_sem=send_sem.at[step, s, offset],
            recv_sem=recv_sem.at[step, s, offset],
            device_id=(gx, (me + offset) % group),
            device_id_type=MESH,
        )

    def slab_copy(step, s, way):
        at = slab_at + way * slab_span
        return pltpu.make_async_remote_copy(
            src_ref=send.at[s, pl.ds(at, slab_span)],
            dst_ref=rems[step % 2][s].at[pl.ds(at, slab_span)],
            send_sem=slab_send_sem.at[step, s, way],
            recv_sem=slab_recv_sem.at[step, s, way],
            device_id=(gx + 1 - 2 * way, me),
            device_id_type=MESH,
        )

    def post_rows(step, s):
        def post(turn, carry):
            offset = 1 + (2 * turn + 1) % (group - 1)
            target = (me + offset) % group
            for p in range(peers):
                row = peer_ref[0, target * peers + p]
                for n in range(kp):
                    send[s, offset * span + p * kp + n] = owns[s][row * kp + n]
            peer_copy(step, s, offset).start()
            return carry

        lax.fori_loop(0, group - 1, post, 0)
        for way, present in enumerate((has_above, has_below)):

            @pl.when(present)
            def _():
                for h in range(halo):
                    row = slab_ref[0, way * halo + h]
                    for n in range(kp):
                        send[s, slab_at + way * slab_span + h * kp + n] = owns[s][row * kp + n]
                slab_copy(step, s, way).start()

        for p in range(peers):
            row = peer_ref[0, me * peers + p]
            for n in range(kp):
                rems[step % 2][s][me * span + p * kp + n] = owns[s][row * kp + n]

    def arrive(step, s):
        def finish(turn, carry):
            peer_copy(step, s, 1 + (2 * turn + 1) % (group - 1)).wait()
            return carry

        lax.fori_loop(0, group - 1, finish, 0)
        for way, (sends, receives) in enumerate(((has_above, has_below), (has_below, has_above))):

            @pl.when(sends)
            def _():
                slab_copy(step, s, way).wait_send()

            @pl.when(receives)
            def _():
                slab_copy(step, s, way).wait_recv()

    def tabulate(row, carry):
        for k in range(kl):
            for n in range(kp):
                match = match_ref[k, n, row]
                table[k, n, row] = jnp.where(
                    match == kp, own_zero, local_ref[k, row] * kp + match
                )
        for k in range(ko):
            source = jnp.maximum(remote_ref[k, row] - rows, 0)
            from_below = (source >= group * peers) & (source < group * peers + halo)
            from_above = source >= group * peers + halo
            missing = (from_below & (gx == 0)) | (from_above & (gx == slabs - 1))
            for n in range(kp):
                match = match_ref[kl + k, n, row]
                table[kl + k, n, row] = jnp.where(
                    (match == kp) | missing, rem_zero, source * kp + match
                )
        return carry

    def product(row, first, last, rows_of):
        blocks = [operator[row, k] for k in range(first, last)]
        picked = [
            side_by_side([rows_of[table[k, n, row]] for n in range(kp)])
            for k in range(first, last)
        ]
        return jnp.dot(
            jnp.concatenate(blocks, axis=1),
            jnp.concatenate(picked, axis=0),
            preferred_element_type=jnp.float32,
        )

    def local_rows(s):
        def local_row(row, carry):
            local_sum[s, row] = product(row, 0, kl, owns[s])
            return carry

        lax.fori_loop(0, rows, local_row, 0)

    def image_of(row, step, s):
        value = local_sum[s, row] + product(row, kl, kl + ko, rems[step % 2][s])
        return value.astype(jnp.bfloat16)

    def smooth_rows(step, s):
        def smooth_row(row, carry):
            update = jnp.dot(
                diagonal[row], image_of(row, step, s), preferred_element_type=jnp.float32
            )
            for n in range(kp):
                before = owns[s][row * kp + n].astype(jnp.float32)
                after = before - update[:, n * columns : (n + 1) * columns]
                owns[s][row * kp + n] = after.astype(jnp.bfloat16)
            return carry

        lax.fori_loop(0, rows, smooth_row, 0)

    def turn_row(row, carry):
        for n in range(kp):
            for s in range(STRIPES):
                turned[row * kp + n, pl.ds(s * columns, columns)] = owns[s][row * kp + n].T
        return carry

    def partial_rows(step, s):
        def partial_row(row, carry):
            image = image_of(row, step, s)
            for n in range(kp):
                blocks = jnp.dot(
                    turned[row * kp + n], image, preferred_element_type=jnp.float32
                ).astype(jnp.bfloat16)
                for m in range(kp):
                    at = (row * kp + n) * kp + m
                    partial[s, at] = blocks[:, m * columns : (m + 1) * columns]
            return carry

        lax.fori_loop(0, rows, partial_row, 0)

    core = me % 2
    half = group * owned // 2
    grain = owned // 2 if owned % 2 == 0 else owned

    def invert(at, carry):
        place = at // owned
        high = place // (group // 2)
        odd = (high + me) % 2
        other = high
        for step in range(1, bits):
            bit = (place >> (bits - 1 - step)) & 1
            other = other | jnp.where(odd == 0, bit << step, bit << (bits - step))
        slot = (me ^ other) * owned + at % owned
        found = count
        for row in range(rows):
            for n in range(kp):
                for m in range(kp):
                    named = (row * kp + n) * kp + m
                    found = jnp.where(slots_ref[n, m, row] == slot, named, found)
        inverse[at] = found
        return carry

    def partner(step):
        def flip(bit):
            return me + bit * (1 - 2 * ((me // bit) % 2))

        if step == 0:
            return flip(1)
        return (1 - core) * flip(1 << step) + core * flip(1 << (bits - step))

    def half_copy(step, s, chunk):
        at = chunk * grain
        if step == 0:
            source = outgoing.at[s, pl.ds(at, grain)]
        else:
            source = total.at[s, pl.ds((half >> step) + at, grain)]
        return pltpu.make_async_remote_copy(
            src_ref=source,
            dst_ref=landed[step].at[s, pl.ds(at, grain)],
            send_sem=half_send_sem.at[step, s, chunk],
            recv_sem=half_recv_sem.at[step, s, chunk],
            device_id=(gx, partner(step)),
            device_id_type=MESH,
        )

    def send_partials(s):
        def send_chunk(turn, carry):
            chunk = half // grain - 1 - turn
            for j in range(grain):
                at = chunk * grain + j
                outgoing[s, at] = partial[s, inverse[half + at]]
            half_copy(0, s, chunk).start()
            return carry

        lax.fori_loop(0, half // grain, send_chunk, 0)

    def add_partials(step, s):
        last = step == bits - 1
        chunks = (half >> step) // grain

        def add(chunk):
            half_copy(step, s, chunk).wait_recv()
            for j in range(grain):
                at = chunk * grain + j
                mine = partial[s, inverse[at]] if step == 0 else total[s, at]
                value = mine.astype(jnp.float32) + landed[step][s, at].astype(jnp.float32)
                if last:
                    coarse_ref[at, :, s * columns : (s + 1) * columns] = value.astype(jnp.bfloat16)
                else:
                    total[s, at] = value.astype(jnp.bfloat16)

        if last:
            for chunk in reversed(range(chunks)):
                add(chunk)
            return

        def upper(turn, carry):
            chunk = chunks - 1 - turn
            add(chunk)
            half_copy(step + 1, s, chunk - chunks // 2).start()
            return carry

        def lower(turn, carry):
            add(chunks // 2 - 1 - turn)
            return carry

        lax.fori_loop(0, chunks // 2, upper, 0)
        lax.fori_loop(0, chunks // 2, lower, 0)

    stripes = range(STRIPES)
    load_peers.wait()
    load_slabs.wait()
    load_rows(0).wait()
    post_rows(0, 0)
    load_matches.wait()
    load_locals.wait()
    load_remotes.wait()
    lax.fori_loop(0, rows, tabulate, 0)
    for s in stripes[1:]:
        load_rows(s).wait()
    load_operator.wait()
    for s in stripes:
        local_rows(s)
    for s in stripes[1:]:
        post_rows(0, s)
    load_slots.wait()
    lax.fori_loop(0, group * owned, invert, 0)
    load_diagonal.wait()

    stores = []
    for step in range(2):
        for s in stripes:
            arrive(step, s)
            smooth_rows(step, s)
            post_rows(step + 1, s)
            if step == 1:
                store = pltpu.make_async_copy(
                    owns[s].at[pl.ds(0, own_zero)],
                    smooth_hbm.at[:, :, pl.ds(s * columns, columns)],
                    out_sem.at[s],
                )
                store.start()
                stores.append(store)
            local_rows(s)
    lax.fori_loop(0, rows, turn_row, 0)

    for s in stripes:
        if s > 0:
            add_partials(0, s - 1)
        arrive(2, s)
        partial_rows(2, s)
        send_partials(s)
    for step in range(1, bits):
        add_partials(step, 0)
        add_partials(step - 1, 1)
    add_partials(bits - 1, 1)
    for s in stripes:
        for step in range(bits):
            for chunk in range((half >> step) // grain):
                half_copy(step, s, chunk).wait_send()
    for store in stores:
        store.wait()


def body(
    operator_blocks,
    local_columns,
    remote_columns,
    match_slots,
    tentative,
    inverse_diagonal,
    peer_sends,
    slab_sends,
    coarse_slots,
):
    slabs = lax.axis_size("gx")
    group = lax.axis_size("gy")
    rows, kp, width = tentative.shape[:3]
    kl, ko = local_columns.shape[1], remote_columns.shape[1]
    peers = peer_sends.shape[1] // group
    halo = slab_sends.shape[1] // 2
    owned = (3 * rows * kp * kp // 2 + group - 1) // group
    bits = group.bit_length() - 1
    count = rows * kp * kp
    columns = width // STRIPES
    dims = (slabs, group, rows, kl, ko, kp, peers, halo, owned)

    def blocks(n):
        return pltpu.VMEM((STRIPES, n, width, columns), jnp.bfloat16)

    tables = (
        local_columns.T,
        remote_columns.T,
        match_slots.transpose(1, 2, 0),
        peer_sends,
        slab_sends,
        coarse_slots.transpose(1, 2, 0),
    )
    arrays = (operator_blocks, tentative.reshape(rows * kp, width, width), inverse_diagonal)
    anywhere = pl.BlockSpec(memory_space=pl.ANY)
    half = group * owned // 2
    remote_count = (group * peers + 2 * halo) * kp
    scratch_blocks = (
        (kl + ko + 1) * rows
        + rows * kp * 2
        + 3 * remote_count
        + 2 * rows * kp
        + count
        + 4 * half
        + owned
        + 4
    )
    grant = scratch_blocks * width * width * 2 + 3_000_000
    smoothed, coarse = pl.pallas_call(
        functools.partial(kernel, dims),
        out_shape=(
            jax.ShapeDtypeStruct((rows * kp, width, width), jnp.bfloat16),
            jax.ShapeDtypeStruct((owned, width, width), jnp.bfloat16),
        ),
        in_specs=[pl.BlockSpec(memory_space=pltpu.HBM)] * 9,
        out_specs=(anywhere, pl.BlockSpec(memory_space=pltpu.VMEM)),
        scratch_shapes=[
            pltpu.VMEM(operator_blocks.shape, jnp.bfloat16),
            pltpu.VMEM((rows, width, width), jnp.bfloat16),
            blocks(remote_count),
            pltpu.VMEM((STRIPES, rows, width, kp * columns), jnp.float32),
            pltpu.VMEM((rows * kp, width, width), jnp.bfloat16),
            blocks(count + 1),
            blocks(half),
            blocks(half),
            *[pltpu.SMEM(table.shape, jnp.int32) for table in tables],
            pltpu.SMEM((kl + ko, kp, rows), jnp.int32),
            pltpu.SMEM((2 * half,), jnp.int32),
            *[pltpu.VMEM((rows * kp + 1, width, columns), jnp.bfloat16)] * STRIPES,
            *[pltpu.VMEM((remote_count + 1, width, columns), jnp.bfloat16)] * (2 * STRIPES),
            *[blocks(half >> step) for step in range(bits)],
            pltpu.SemaphoreType.DMA((len(tables),)),
            pltpu.SemaphoreType.DMA((2,)),
            pltpu.SemaphoreType.DMA((STRIPES,)),
            pltpu.SemaphoreType.DMA((STRIPES,)),
            pltpu.SemaphoreType.DMA((3, STRIPES, group)),
            pltpu.SemaphoreType.DMA((3, STRIPES, group)),
            pltpu.SemaphoreType.DMA((3, STRIPES, 2)),
            pltpu.SemaphoreType.DMA((3, STRIPES, 2)),
            pltpu.SemaphoreType.DMA((bits, STRIPES, group)),
            pltpu.SemaphoreType.DMA((bits, STRIPES, group)),
        ],
        compiler_params=pltpu.CompilerParams(
            collective_id=0, has_side_effects=True, vmem_limit_bytes=grant
        ),
    )(*[pltpu.with_memory_space_constraint(x, pltpu.HBM) for x in tables + arrays])
    return smoothed.reshape(tentative.shape), coarse


def solution(mesh):
    placed = (
        P(("gx", "gy"), None, None, None),
        P(("gx", "gy"), None),
        P(("gx", "gy"), None),
        P(("gx", "gy"), None, None),
        P(("gx", "gy"), None, None, None),
        P(("gx", "gy"), None, None),
        P(("gx", "gy"), None),
        P(("gx", "gy"), None),
        P(("gx", "gy"), None, None),
    )
    return jax.shard_map(
        body,
        mesh=mesh,
        in_specs=placed,
        out_specs=(P(("gx", "gy"), None, None, None), P(("gx", "gy"), None, None)),
        check_vma=False,
    )
```

```python
import functools

import jax
import jax.numpy as jnp
from jax import lax
from jax.experimental import pallas as pl
from jax.experimental.pallas import tpu as pltpu
from jax.sharding import PartitionSpec as P

MESH = pl.DeviceIdType.MESH
STRIPES = 2


def side_by_side(parts):
    return parts[0] if len(parts) == 1 else jnp.concatenate(parts, axis=1)


def kernel(
    dims,
    local_hbm,
    remote_hbm,
    match_hbm,
    peer_hbm,
    slab_hbm,
    slots_hbm,
    operator_hbm,
    tentative_hbm,
    diagonal_hbm,
    smooth_hbm,
    coarse_ref,
    operator,
    diagonal,
    send,
    local_sum,
    turned,
    partial,
    outgoing,
    total,
    local_ref,
    remote_ref,
    match_ref,
    peer_ref,
    slab_ref,
    slots_ref,
    table,
    inverse,
    *rest,
):
    slabs, group, rows, kl, ko, kp, peers, halo, owned = dims
    bits = group.bit_length() - 1
    owns, rest = rest[:STRIPES], rest[STRIPES:]
    rems, rest = (rest[:STRIPES], rest[STRIPES : 2 * STRIPES]), rest[2 * STRIPES :]
    landed = rest[:bits]
    (
        index_sem,
        load_sem,
        rows_sem,
        out_sem,
        send_sem,
        recv_sem,
        slab_send_sem,
        slab_recv_sem,
        half_send_sem,
        half_recv_sem,
    ) = rest[bits:]
    width = operator.shape[-1]
    columns = width // STRIPES
    gx = lax.axis_index("gx")
    me = lax.axis_index("gy")
    has_below = gx > 0
    has_above = gx < slabs - 1
    own_zero = rows * kp
    rem_zero = (group * peers + 2 * halo) * kp
    count = rows * kp * kp
    span = peers * kp
    slab_span = halo * kp
    slab_at = group * span

    def load_rows(s):
        return pltpu.make_async_copy(
            tentative_hbm.at[:, :, pl.ds(s * columns, columns)],
            owns[s].at[pl.ds(0, own_zero)],
            rows_sem.at[s],
        )

    load_peers = pltpu.make_async_copy(peer_hbm, peer_ref, index_sem.at[0])
    load_slabs = pltpu.make_async_copy(slab_hbm, slab_ref, index_sem.at[1])
    load_matches = pltpu.make_async_copy(match_hbm, match_ref, index_sem.at[2])
    load_locals = pltpu.make_async_copy(local_hbm, local_ref, index_sem.at[3])
    load_remotes = pltpu.make_async_copy(remote_hbm, remote_ref, index_sem.at[4])
    load_slots = pltpu.make_async_copy(slots_hbm, slots_ref, index_sem.at[5])
    load_rows(0).start()
    for load in (load_peers, load_slabs, load_matches, load_locals, load_remotes, load_slots):
        load.start()
    for s in range(1, STRIPES):
        load_rows(s).start()
    load_operator = pltpu.make_async_copy(operator_hbm, operator, load_sem.at[0])
    load_operator.start()
    load_diagonal = pltpu.make_async_copy(diagonal_hbm, diagonal, load_sem.at[1])
    load_diagonal.start()

    barrier = pltpu.get_barrier_semaphore()

    def greet(offset, carry):
        pl.semaphore_signal(
            barrier, inc=1, device_id=(gx, (me + offset) % group), device_id_type=MESH
        )
        return carry

    lax.fori_loop(1, group, greet, 0)

    @pl.when(has_below)
    def _():
        pl.semaphore_signal(barrier, inc=1, device_id=(gx - 1, me), device_id_type=MESH)

    @pl.when(has_above)
    def _():
        pl.semaphore_signal(barrier, inc=1, device_id=(gx + 1, me), device_id_type=MESH)

    zero = jnp.zeros((width, columns), jnp.bfloat16)
    for s in range(STRIPES):
        owns[s][own_zero] = zero
        for rem in rems:
            rem[s][rem_zero] = zero
        partial[s, count] = zero
    neighbours = jnp.where(has_below, 1, 0) + jnp.where(has_above, 1, 0)
    pl.semaphore_wait(barrier, group - 1 + neighbours)

    def peer_copy(step, s, offset):
        return pltpu.make_async_remote_copy(
            src_ref=send.at[s, pl.ds(offset * span, span)],
            dst_ref=rems[step % 2][s].at[pl.ds(me * span, span)],
            send_sem=send_sem.at[step, s, offset],
            recv_sem=recv_sem.at[step, s, offset],
            device_id=(gx, (me + offset) % group),
            device_id_type=MESH,
        )

    def slab_copy(step, s, way):
        at = slab_at + way * slab_span
        return pltpu.make_async_remote_copy(
            src_ref=send.at[s, pl.ds(at, slab_span)],
            dst_ref=rems[step % 2][s].at[pl.ds(at, slab_span)],
            send_sem=slab_send_sem.at[step, s, way],
            recv_sem=slab_recv_sem.at[step, s, way],
            device_id=(gx + 1 - 2 * way, me),
            device_id_type=MESH,
        )

    def post_rows(step, s):
        def post(turn, carry):
            offset = 1 + (turn + 5) % (group - 1)
            target = (me + offset) % group
            for p in range(peers):
                row = peer_ref[0, target * peers + p]
                for n in range(kp):
                    send[s, offset * span + p * kp + n] = owns[s][row * kp + n]
            peer_copy(step, s, offset).start()
            return carry

        lax.fori_loop(0, group - 1, post, 0)
        for way, present in enumerate((has_above, has_below)):

            @pl.when(present)
            def _():
                for h in range(halo):
                    row = slab_ref[0, way * halo + h]
                    for n in range(kp):
                        send[s, slab_at + way * slab_span + h * kp + n] = owns[s][row * kp + n]
                slab_copy(step, s, way).start()

        for p in range(peers):
            row = peer_ref[0, me * peers + p]
            for n in range(kp):
                rems[step % 2][s][me * span + p * kp + n] = owns[s][row * kp + n]

    def arrive(step, s):
        def finish(turn, carry):
            peer_copy(step, s, 1 + (turn + 5) % (group - 1)).wait()
            return carry

        lax.fori_loop(0, group - 1, finish, 0)
        for way, (sends, receives) in enumerate(((has_above, has_below), (has_below, has_above))):

            @pl.when(sends)
            def _():
                slab_copy(step, s, way).wait_send()

            @pl.when(receives)
            def _():
                slab_copy(step, s, way).wait_recv()

    def tabulate(row, carry):
        for k in range(kl):
            for n in range(kp):
                match = match_ref[k, n, row]
                table[k, n, row] = jnp.where(
                    match == kp, own_zero, local_ref[k, row] * kp + match
                )
        for k in range(ko):
            source = jnp.maximum(remote_ref[k, row] - rows, 0)
            from_below = (source >= group * peers) & (source < group * peers + halo)
            from_above = source >= group * peers + halo
            missing = (from_below & (gx == 0)) | (from_above & (gx == slabs - 1))
            for n in range(kp):
                match = match_ref[kl + k, n, row]
                table[kl + k, n, row] = jnp.where(
                    (match == kp) | missing, rem_zero, source * kp + match
                )
        return carry

    def product(row, first, last, rows_of):
        blocks = [operator[row, k] for k in range(first, last)]
        picked = [
            side_by_side([rows_of[table[k, n, row]] for n in range(kp)])
            for k in range(first, last)
        ]
        return jnp.dot(
            jnp.concatenate(blocks, axis=1),
            jnp.concatenate(picked, axis=0),
            preferred_element_type=jnp.float32,
        )

    def local_rows(s):
        def local_row(row, carry):
            local_sum[s, row] = product(row, 0, kl, owns[s])
            return carry

        lax.fori_loop(0, rows, local_row, 0)

    def image_of(row, step, s):
        value = local_sum[s, row] + product(row, kl, kl + ko, rems[step % 2][s])
        return value.astype(jnp.bfloat16)

    def smooth_rows(step, s):
        def smooth_row(row, carry):
            update = jnp.dot(
                diagonal[row], image_of(row, step, s), preferred_element_type=jnp.float32
            )
            for n in range(kp):
                before = owns[s][row * kp + n].astype(jnp.float32)
                after = before - update[:, n * columns : (n + 1) * columns]
                owns[s][row * kp + n] = after.astype(jnp.bfloat16)
            return carry

        lax.fori_loop(0, rows, smooth_row, 0)

    def turn_row(row, carry):
        for n in range(kp):
            for s in range(STRIPES):
                turned[row * kp + n, pl.ds(s * columns, columns)] = owns[s][row * kp + n].T
        return carry

    def partial_rows(step, s):
        def partial_row(row, carry):
            image = image_of(row, step, s)
            for n in range(kp):
                blocks = jnp.dot(
                    turned[row * kp + n], image, preferred_element_type=jnp.float32
                ).astype(jnp.bfloat16)
                for m in range(kp):
                    at = (row * kp + n) * kp + m
                    partial[s, at] = blocks[:, m * columns : (m + 1) * columns]
            return carry

        lax.fori_loop(0, rows, partial_row, 0)

    core = me % 2
    half = group * owned // 2
    grain = owned

    def invert(at, carry):
        place = at // owned
        high = place // (group // 2)
        odd = (high + me) % 2
        other = high
        for step in range(1, bits):
            bit = (place >> (bits - 1 - step)) & 1
            other = other | jnp.where(odd == 0, bit << step, bit << (bits - step))
        slot = (me ^ other) * owned + at % owned
        found = count
        for row in range(rows):
            for n in range(kp):
                for m in range(kp):
                    named = (row * kp + n) * kp + m
                    found = jnp.where(slots_ref[n, m, row] == slot, named, found)
        inverse[at] = found
        return carry

    def partner(step):
        def flip(bit):
            return me + bit * (1 - 2 * ((me // bit) % 2))

        if step == 0:
            return flip(1)
        return (1 - core) * flip(1 << step) + core * flip(1 << (bits - step))

    def half_copy(step, s, chunk):
        at = chunk * grain
        if step == 0:
            source = outgoing.at[s, pl.ds(at, grain)]
        else:
            source = total.at[s, pl.ds((half >> step) + at, grain)]
        return pltpu.make_async_remote_copy(
            src_ref=source,
            dst_ref=landed[step].at[s, pl.ds(at, grain)],
            send_sem=half_send_sem.at[step, s, chunk],
            recv_sem=half_recv_sem.at[step, s, chunk],
            device_id=(gx, partner(step)),
            device_id_type=MESH,
        )

    def send_partials(s):
        def send_chunk(turn, carry):
            chunk = half // grain - 1 - turn
            for j in range(grain):
                at = chunk * grain + j
                outgoing[s, at] = partial[s, inverse[half + at]]
            half_copy(0, s, chunk).start()
            return carry

        lax.fori_loop(0, half // grain, send_chunk, 0)

    def add_partials(step, s):
        last = step == bits - 1
        chunks = (half >> step) // grain

        def add(chunk):
            half_copy(step, s, chunk).wait_recv()
            for j in range(grain):
                at = chunk * grain + j
                mine = partial[s, inverse[at]] if step == 0 else total[s, at]
                value = mine.astype(jnp.float32) + landed[step][s, at].astype(jnp.float32)
                if last:
                    coarse_ref[at, :, s * columns : (s + 1) * columns] = value.astype(jnp.bfloat16)
                else:
                    total[s, at] = value.astype(jnp.bfloat16)

        if last:
            for chunk in reversed(range(chunks)):
                add(chunk)
            return

        def upper(turn, carry):
            chunk = chunks - 1 - turn
            add(chunk)
            half_copy(step + 1, s, chunk - chunks // 2).start()
            return carry

        def lower(turn, carry):
            add(chunks // 2 - 1 - turn)
            return carry

        lax.fori_loop(0, chunks // 2, upper, 0)
        lax.fori_loop(0, chunks // 2, lower, 0)

    stripes = range(STRIPES)
    load_peers.wait()
    load_slabs.wait()
    load_rows(0).wait()
    post_rows(0, 0)
    load_matches.wait()
    load_locals.wait()
    load_remotes.wait()
    lax.fori_loop(0, rows, tabulate, 0)
    for s in stripes[1:]:
        load_rows(s).wait()
    load_operator.wait()
    for s in stripes:
        local_rows(s)
    for s in stripes[1:]:
        post_rows(0, s)
    load_slots.wait()
    lax.fori_loop(0, group * owned, invert, 0)
    load_diagonal.wait()

    stores = []
    for step in range(2):
        for s in stripes:
            arrive(step, s)
            smooth_rows(step, s)
            post_rows(step + 1, s)
            if step == 1:
                store = pltpu.make_async_copy(
                    owns[s].at[pl.ds(0, own_zero)],
                    smooth_hbm.at[:, :, pl.ds(s * columns, columns)],
                    out_sem.at[s],
                )
                store.start()
                stores.append(store)
            local_rows(s)
    lax.fori_loop(0, rows, turn_row, 0)

    for s in stripes:
        if s > 0:
            add_partials(0, s - 1)
        arrive(2, s)
        partial_rows(2, s)
        send_partials(s)
    for step in range(1, bits):
        add_partials(step, 0)
        add_partials(step - 1, 1)
    add_partials(bits - 1, 1)
    for s in stripes:
        for step in range(bits):
            for chunk in range((half >> step) // grain):
                half_copy(step, s, chunk).wait_send()
    for store in stores:
        store.wait()


def deliver(pieces, smooth_ref, coarse_ref, smooth_out, coarse_out, sem):
    copies = []
    for which, (source, target) in enumerate(((smooth_ref, smooth_out), (coarse_ref, coarse_out))):
        step = pl.cdiv(source.shape[0], pieces)
        for piece, at in enumerate(range(0, source.shape[0], step)):
            window = pl.ds(at, min(step, source.shape[0] - at))
            copies.append(
                pltpu.make_async_copy(
                    source.at[window], target.at[window], sem.at[which, piece]
                )
            )
    for copy in copies:
        copy.start()
    for copy in copies:
        copy.wait()


def body(
    operator_blocks,
    local_columns,
    remote_columns,
    match_slots,
    tentative,
    inverse_diagonal,
    peer_sends,
    slab_sends,
    coarse_slots,
):
    slabs = lax.axis_size("gx")
    group = lax.axis_size("gy")
    rows, kp, width = tentative.shape[:3]
    kl, ko = local_columns.shape[1], remote_columns.shape[1]
    peers = peer_sends.shape[1] // group
    halo = slab_sends.shape[1] // 2
    owned = (3 * rows * kp * kp // 2 + group - 1) // group
    bits = group.bit_length() - 1
    count = rows * kp * kp
    columns = width // STRIPES
    dims = (slabs, group, rows, kl, ko, kp, peers, halo, owned)

    def blocks(n):
        return pltpu.VMEM((STRIPES, n, width, columns), jnp.bfloat16)

    tables = (
        local_columns.T,
        remote_columns.T,
        match_slots.transpose(1, 2, 0),
        peer_sends,
        slab_sends,
        coarse_slots.transpose(1, 2, 0),
    )
    arrays = (operator_blocks, tentative.reshape(rows * kp, width, width), inverse_diagonal)
    anywhere = pl.BlockSpec(memory_space=pl.ANY)
    half = group * owned // 2
    remote_count = (group * peers + 2 * halo) * kp
    scratch_blocks = (
        (kl + ko + 1) * rows
        + rows * kp * 2
        + 3 * remote_count
        + 2 * rows * kp
        + count
        + 4 * half
        + owned
        + 4
    )
    grant = scratch_blocks * width * width * 2 + 3_000_000
    smoothed, coarse = pl.pallas_call(
        functools.partial(kernel, dims),
        out_shape=(
            jax.ShapeDtypeStruct((rows * kp, width, width), jnp.bfloat16),
            jax.ShapeDtypeStruct((owned, width, width), jnp.bfloat16),
        ),
        in_specs=[pl.BlockSpec(memory_space=pltpu.HBM)] * 9,
        out_specs=(anywhere, pl.BlockSpec(memory_space=pltpu.VMEM)),
        scratch_shapes=[
            pltpu.VMEM(operator_blocks.shape, jnp.bfloat16),
            pltpu.VMEM((rows, width, width), jnp.bfloat16),
            blocks(remote_count),
            pltpu.VMEM((STRIPES, rows, width, kp * columns), jnp.float32),
            pltpu.VMEM((rows * kp, width, width), jnp.bfloat16),
            blocks(count + 1),
            blocks(half),
            blocks(half),
            *[pltpu.SMEM(table.shape, jnp.int32) for table in tables],
            pltpu.SMEM((kl + ko, kp, rows), jnp.int32),
            pltpu.SMEM((2 * half,), jnp.int32),
            *[pltpu.VMEM((rows * kp + 1, width, columns), jnp.bfloat16)] * STRIPES,
            *[pltpu.VMEM((remote_count + 1, width, columns), jnp.bfloat16)] * (2 * STRIPES),
            *[blocks(half >> step) for step in range(bits)],
            pltpu.SemaphoreType.DMA((len(tables),)),
            pltpu.SemaphoreType.DMA((2,)),
            pltpu.SemaphoreType.DMA((STRIPES,)),
            pltpu.SemaphoreType.DMA((STRIPES,)),
            pltpu.SemaphoreType.DMA((3, STRIPES, group)),
            pltpu.SemaphoreType.DMA((3, STRIPES, group)),
            pltpu.SemaphoreType.DMA((3, STRIPES, 2)),
            pltpu.SemaphoreType.DMA((3, STRIPES, 2)),
            pltpu.SemaphoreType.DMA((bits, STRIPES, group)),
            pltpu.SemaphoreType.DMA((bits, STRIPES, group)),
        ],
        compiler_params=pltpu.CompilerParams(
            collective_id=0, has_side_effects=True, vmem_limit_bytes=grant
        ),
    )(*[pltpu.with_memory_space_constraint(x, pltpu.HBM) for x in tables + arrays])
    pieces = 4
    results = [pltpu.with_memory_space_constraint(x, pltpu.VMEM) for x in (smoothed, coarse)]
    smoothed, coarse = pl.pallas_call(
        functools.partial(deliver, pieces),
        out_shape=tuple(jax.ShapeDtypeStruct(x.shape, x.dtype) for x in (smoothed, coarse)),
        in_specs=[pl.BlockSpec(memory_space=pltpu.VMEM)] * 2,
        out_specs=(anywhere, anywhere),
        scratch_shapes=[pltpu.SemaphoreType.DMA((2, pieces))],
    )(*results)
    return smoothed.reshape(tentative.shape), coarse


def solution(mesh):
    placed = (
        P(("gx", "gy"), None, None, None),
        P(("gx", "gy"), None),
        P(("gx", "gy"), None),
        P(("gx", "gy"), None, None),
        P(("gx", "gy"), None, None, None),
        P(("gx", "gy"), None, None),
        P(("gx", "gy"), None),
        P(("gx", "gy"), None),
        P(("gx", "gy"), None, None),
    )
    return jax.shard_map(
        body,
        mesh=mesh,
        in_specs=placed,
        out_specs=(P(("gx", "gy"), None, None, None), P(("gx", "gy"), None, None)),
        check_vma=False,
    )
```

```python
import functools
import math

import jax
import jax.numpy as jnp
from jax import lax
from jax.experimental import pallas as pl
from jax.experimental.pallas import tpu as pltpu
from jax.sharding import PartitionSpec as P

MESH = pl.DeviceIdType.MESH
STRIPES = 2


def side_by_side(parts):
    return parts[0] if len(parts) == 1 else jnp.concatenate(parts, axis=1)


def kernel(
    dims,
    local_hbm,
    remote_hbm,
    match_hbm,
    peer_hbm,
    slab_hbm,
    slots_hbm,
    operator_hbm,
    tentative_hbm,
    diagonal_hbm,
    smooth_hbm,
    coarse_ref,
    operator,
    diagonal,
    send,
    local_sum,
    turned,
    partial,
    outgoing,
    total,
    local_ref,
    remote_ref,
    match_ref,
    peer_ref,
    slab_ref,
    slots_ref,
    table,
    inverse,
    *rest,
):
    slabs, group, rows, kl, ko, kp, peers, halo, owned = dims
    bits = group.bit_length() - 1
    owns, rest = rest[:STRIPES], rest[STRIPES:]
    rems, rest = (rest[:STRIPES], rest[STRIPES : 2 * STRIPES]), rest[2 * STRIPES :]
    landed = rest[:bits]
    (
        index_sem,
        load_sem,
        rows_sem,
        out_sem,
        send_sem,
        recv_sem,
        slab_send_sem,
        slab_recv_sem,
        half_send_sem,
        half_recv_sem,
    ) = rest[bits:]
    width = operator.shape[-1]
    columns = width // STRIPES
    gx = lax.axis_index("gx")
    me = lax.axis_index("gy")
    has_below = gx > 0
    has_above = gx < slabs - 1
    own_zero = rows * kp
    rem_zero = (group * peers + 2 * halo) * kp
    count = rows * kp * kp
    span = peers * kp
    slab_span = halo * kp
    slab_at = group * span

    def load_rows(s):
        return pltpu.make_async_copy(
            tentative_hbm.at[:, :, pl.ds(s * columns, columns)],
            owns[s].at[pl.ds(0, own_zero)],
            rows_sem.at[s],
        )

    load_peers = pltpu.make_async_copy(peer_hbm, peer_ref, index_sem.at[0])
    load_slabs = pltpu.make_async_copy(slab_hbm, slab_ref, index_sem.at[1])
    load_matches = pltpu.make_async_copy(match_hbm, match_ref, index_sem.at[2])
    load_locals = pltpu.make_async_copy(local_hbm, local_ref, index_sem.at[3])
    load_remotes = pltpu.make_async_copy(remote_hbm, remote_ref, index_sem.at[4])
    load_slots = pltpu.make_async_copy(slots_hbm, slots_ref, index_sem.at[5])
    load_rows(0).start()
    load_peers.start()
    load_slabs.start()

    barrier = pltpu.get_barrier_semaphore()

    def greet(offset, carry):
        pl.semaphore_signal(
            barrier, inc=1, device_id=(gx, (me + offset) % group), device_id_type=MESH
        )
        return carry

    lax.fori_loop(1, group, greet, 0)

    @pl.when(has_below)
    def _():
        pl.semaphore_signal(barrier, inc=1, device_id=(gx - 1, me), device_id_type=MESH)

    @pl.when(has_above)
    def _():
        pl.semaphore_signal(barrier, inc=1, device_id=(gx + 1, me), device_id_type=MESH)

    for s in range(1, STRIPES):
        load_rows(s).start()
    for load in (load_matches, load_locals, load_remotes, load_slots):
        load.start()
    load_operator = pltpu.make_async_copy(operator_hbm, operator, load_sem.at[0])
    load_operator.start()
    load_diagonal = pltpu.make_async_copy(diagonal_hbm, diagonal, load_sem.at[1])
    load_diagonal.start()
    neighbours = jnp.where(has_below, 1, 0) + jnp.where(has_above, 1, 0)
    pl.semaphore_wait(barrier, group - 1 + neighbours)

    def peer_copy(step, s, offset):
        return pltpu.make_async_remote_copy(
            src_ref=send.at[s, pl.ds(offset * span, span)],
            dst_ref=rems[step % 2][s].at[pl.ds(me * span, span)],
            send_sem=send_sem.at[step, s, offset],
            recv_sem=recv_sem.at[step, s, offset],
            device_id=(gx, (me + offset) % group),
            device_id_type=MESH,
        )

    def slab_copy(step, s, way):
        at = slab_at + way * slab_span
        return pltpu.make_async_remote_copy(
            src_ref=send.at[s, pl.ds(at, slab_span)],
            dst_ref=rems[step % 2][s].at[pl.ds(at, slab_span)],
            send_sem=slab_send_sem.at[step, s, way],
            recv_sem=slab_recv_sem.at[step, s, way],
            device_id=(gx + 1 - 2 * way, me),
            device_id_type=MESH,
        )

    def post_rows(step, s):
        def post(turn, carry):
            offset = 1 + (turn + 5) % (group - 1)
            target = (me + offset) % group
            for p in range(peers):
                row = peer_ref[0, target * peers + p]
                for n in range(kp):
                    send[s, offset * span + p * kp + n] = owns[s][row * kp + n]
            peer_copy(step, s, offset).start()
            return carry

        lax.fori_loop(0, group - 1, post, 0)
        for way, present in enumerate((has_above, has_below)):

            @pl.when(present)
            def _():
                for h in range(halo):
                    row = slab_ref[0, way * halo + h]
                    for n in range(kp):
                        send[s, slab_at + way * slab_span + h * kp + n] = owns[s][row * kp + n]
                slab_copy(step, s, way).start()

        for p in range(peers):
            row = peer_ref[0, me * peers + p]
            for n in range(kp):
                rems[step % 2][s][me * span + p * kp + n] = owns[s][row * kp + n]

    def arrive(step, s):
        def finish(turn, carry):
            peer_copy(step, s, 1 + (turn + 5) % (group - 1)).wait()
            return carry

        lax.fori_loop(0, group - 1, finish, 0)
        for way, (sends, receives) in enumerate(((has_above, has_below), (has_below, has_above))):

            @pl.when(sends)
            def _():
                slab_copy(step, s, way).wait_send()

            @pl.when(receives)
            def _():
                slab_copy(step, s, way).wait_recv()

    def tabulate(row, carry):
        for k in range(kl):
            for n in range(kp):
                match = match_ref[k, n, row]
                table[k, n, row] = jnp.where(
                    match == kp, own_zero, local_ref[k, row] * kp + match
                )
        for k in range(ko):
            source = jnp.maximum(remote_ref[k, row] - rows, 0)
            from_below = (source >= group * peers) & (source < group * peers + halo)
            from_above = source >= group * peers + halo
            missing = (from_below & (gx == 0)) | (from_above & (gx == slabs - 1))
            for n in range(kp):
                match = match_ref[kl + k, n, row]
                table[kl + k, n, row] = jnp.where(
                    (match == kp) | missing, rem_zero, source * kp + match
                )
        return carry

    def product(row, first, last, rows_of):
        blocks = [operator[row, k] for k in range(first, last)]
        picked = [
            side_by_side([rows_of[table[k, n, row]] for n in range(kp)])
            for k in range(first, last)
        ]
        return jnp.dot(
            jnp.concatenate(blocks, axis=1),
            jnp.concatenate(picked, axis=0),
            preferred_element_type=jnp.float32,
        )

    def local_rows(s):
        def local_row(row, carry):
            local_sum[s, row] = product(row, 0, kl, owns[s])
            return carry

        lax.fori_loop(0, rows, local_row, 0)

    def image_of(row, step, s):
        value = local_sum[s, row] + product(row, kl, kl + ko, rems[step % 2][s])
        return value.astype(jnp.bfloat16)

    def smooth_rows(step, s):
        def smooth_row(row, carry):
            update = jnp.dot(
                diagonal[row], image_of(row, step, s), preferred_element_type=jnp.float32
            )
            for n in range(kp):
                before = owns[s][row * kp + n].astype(jnp.float32)
                after = before - update[:, n * columns : (n + 1) * columns]
                owns[s][row * kp + n] = after.astype(jnp.bfloat16)
            return carry

        lax.fori_loop(0, rows, smooth_row, 0)

    def turn_row(row, carry):
        for n in range(kp):
            for s in range(STRIPES):
                turned[row, pl.ds(n * width + s * columns, columns)] = owns[s][row * kp + n].T
        return carry

    def partial_rows(step, s):
        def partial_row(row, carry):
            image = image_of(row, step, s)
            stack = jnp.dot(turned[row], image, preferred_element_type=jnp.float32)
            for n in range(kp):
                blocks = stack[n * width : (n + 1) * width].astype(jnp.bfloat16)
                for m in range(kp):
                    at = (row * kp + n) * kp + m
                    partial[s, at] = blocks[:, m * columns : (m + 1) * columns]
            return carry

        lax.fori_loop(0, rows, partial_row, 0)

    core = me % 2
    half = group * owned // 2
    grain = owned

    def invert(at, carry):
        place = at // owned
        high = place // (group // 2)
        odd = (high + me) % 2
        other = high
        for step in range(1, bits):
            bit = (place >> (bits - 1 - step)) & 1
            other = other | jnp.where(odd == 0, bit << step, bit << (bits - step))
        slot = (me ^ other) * owned + at % owned
        found = count
        for row in range(rows):
            for n in range(kp):
                for m in range(kp):
                    named = (row * kp + n) * kp + m
                    found = jnp.where(slots_ref[n, m, row] == slot, named, found)
        inverse[at] = found
        return carry

    def partner(step):
        def flip(bit):
            return me + bit * (1 - 2 * ((me // bit) % 2))

        if step == 0:
            return flip(1)
        return (1 - core) * flip(1 << step) + core * flip(1 << (bits - step))

    def half_copy(step, s, chunk):
        at = chunk * grain
        if step == 0:
            source = outgoing.at[s, pl.ds(at, grain)]
        else:
            source = total.at[s, pl.ds((half >> step) + at, grain)]
        return pltpu.make_async_remote_copy(
            src_ref=source,
            dst_ref=landed[step].at[s, pl.ds(at, grain)],
            send_sem=half_send_sem.at[step, s, chunk],
            recv_sem=half_recv_sem.at[step, s, chunk],
            device_id=(gx, partner(step)),
            device_id_type=MESH,
        )

    def send_partials(s):
        def send_chunk(turn, carry):
            chunk = half // grain - 1 - turn
            for j in range(grain):
                at = chunk * grain + j
                outgoing[s, at] = partial[s, inverse[half + at]]
            half_copy(0, s, chunk).start()
            return carry

        lax.fori_loop(0, half // grain, send_chunk, 0)

    def add_partials(step, s):
        last = step == bits - 1
        chunks = (half >> step) // grain

        def add(chunk):
            half_copy(step, s, chunk).wait_recv()
            for j in range(grain):
                at = chunk * grain + j
                mine = partial[s, inverse[at]] if step == 0 else total[s, at]
                value = mine.astype(jnp.float32) + landed[step][s, at].astype(jnp.float32)
                if last:
                    coarse_ref[at, :, s * columns : (s + 1) * columns] = value.astype(jnp.bfloat16)
                else:
                    total[s, at] = value.astype(jnp.bfloat16)

        if last:
            for chunk in reversed(range(chunks)):
                add(chunk)
            return

        def upper(turn, carry):
            chunk = chunks - 1 - turn
            add(chunk)
            half_copy(step + 1, s, chunk - chunks // 2).start()
            return carry

        def lower(turn, carry):
            add(chunks // 2 - 1 - turn)
            return carry

        lax.fori_loop(0, chunks // 2, upper, 0)
        lax.fori_loop(0, chunks // 2, lower, 0)

    stripes = range(STRIPES)
    load_peers.wait()
    load_slabs.wait()
    load_rows(0).wait()
    post_rows(0, 0)
    zero = jnp.zeros((width, columns), jnp.bfloat16)
    for s in range(STRIPES):
        owns[s][own_zero] = zero
        for rem in rems:
            rem[s][rem_zero] = zero
        partial[s, count] = zero
    load_matches.wait()
    load_locals.wait()
    load_remotes.wait()
    lax.fori_loop(0, rows, tabulate, 0)
    for s in stripes[1:]:
        load_rows(s).wait()
    load_operator.wait()
    for s in stripes:
        local_rows(s)
    for s in stripes[1:]:
        post_rows(0, s)
    load_slots.wait()
    lax.fori_loop(0, group * owned, invert, 0)
    load_diagonal.wait()

    stores = []
    for step in range(2):
        for s in stripes:
            arrive(step, s)
            smooth_rows(step, s)
            post_rows(step + 1, s)
            if step == 1:
                store = pltpu.make_async_copy(
                    owns[s].at[pl.ds(0, own_zero)],
                    smooth_hbm.at[:, :, pl.ds(s * columns, columns)],
                    out_sem.at[s],
                )
                store.start()
                stores.append(store)
            local_rows(s)
    lax.fori_loop(0, rows, turn_row, 0)

    for s in stripes:
        if s > 0:
            add_partials(0, s - 1)
        arrive(2, s)
        partial_rows(2, s)
        send_partials(s)
    for step in range(1, bits):
        add_partials(step, 0)
        add_partials(step - 1, 1)
    add_partials(bits - 1, 1)
    for s in stripes:
        for step in range(bits):
            for chunk in range((half >> step) // grain):
                half_copy(step, s, chunk).wait_send()
    for store in stores:
        store.wait()


def deliver(pieces, smooth_ref, coarse_ref, smooth_out, coarse_out, sem):
    copies = []
    for which, (source, target) in enumerate(((smooth_ref, smooth_out), (coarse_ref, coarse_out))):
        step = pl.cdiv(source.shape[0], pieces)
        for piece, at in enumerate(range(0, source.shape[0], step)):
            window = pl.ds(at, min(step, source.shape[0] - at))
            copies.append(
                pltpu.make_async_copy(
                    source.at[window], target.at[window], sem.at[which, piece]
                )
            )
    for copy in copies:
        copy.start()
    for copy in copies:
        copy.wait()


def body(
    operator_blocks,
    local_columns,
    remote_columns,
    match_slots,
    tentative,
    inverse_diagonal,
    peer_sends,
    slab_sends,
    coarse_slots,
):
    slabs = lax.axis_size("gx")
    group = lax.axis_size("gy")
    rows, kp, width = tentative.shape[:3]
    kl, ko = local_columns.shape[1], remote_columns.shape[1]
    peers = peer_sends.shape[1] // group
    halo = slab_sends.shape[1] // 2
    owned = (3 * rows * kp * kp // 2 + group - 1) // group
    bits = group.bit_length() - 1
    count = rows * kp * kp
    columns = width // STRIPES
    dims = (slabs, group, rows, kl, ko, kp, peers, halo, owned)

    def blocks(n):
        return pltpu.VMEM((STRIPES, n, width, columns), jnp.bfloat16)

    tables = (
        local_columns.T,
        remote_columns.T,
        match_slots.transpose(1, 2, 0),
        peer_sends,
        slab_sends,
        coarse_slots.transpose(1, 2, 0),
    )
    arrays = (operator_blocks, tentative.reshape(rows * kp, width, width), inverse_diagonal)
    anywhere = pl.BlockSpec(memory_space=pl.ANY)
    half = group * owned // 2
    remote_count = (group * peers + 2 * halo) * kp
    vmem = [
        pltpu.VMEM(operator_blocks.shape, jnp.bfloat16),
        pltpu.VMEM((rows, width, width), jnp.bfloat16),
        blocks(remote_count),
        pltpu.VMEM((STRIPES, rows, width, kp * columns), jnp.float32),
        pltpu.VMEM((rows, kp * width, width), jnp.bfloat16),
        blocks(count + 1),
        blocks(half),
        blocks(half),
    ]
    striped = [pltpu.VMEM((rows * kp + 1, width, columns), jnp.bfloat16)] * STRIPES
    striped += [pltpu.VMEM((remote_count + 1, width, columns), jnp.bfloat16)] * (2 * STRIPES)
    landed = [blocks(half >> step) for step in range(bits)]
    used = sum(
        math.prod(x.shape) * jnp.dtype(x.dtype).itemsize for x in [*vmem, *striped, *landed]
    )
    grant = used + owned * width * width * 2 + (1 << 20)
    smoothed, coarse = pl.pallas_call(
        functools.partial(kernel, dims),
        out_shape=(
            jax.ShapeDtypeStruct((rows * kp, width, width), jnp.bfloat16),
            jax.ShapeDtypeStruct((owned, width, width), jnp.bfloat16),
        ),
        in_specs=[pl.BlockSpec(memory_space=pltpu.HBM)] * 9,
        out_specs=(anywhere, pl.BlockSpec(memory_space=pltpu.VMEM)),
        scratch_shapes=[
            *vmem,
            *[pltpu.SMEM(table.shape, jnp.int32) for table in tables],
            pltpu.SMEM((kl + ko, kp, rows), jnp.int32),
            pltpu.SMEM((2 * half,), jnp.int32),
            *striped,
            *landed,
            pltpu.SemaphoreType.DMA((len(tables),)),
            pltpu.SemaphoreType.DMA((2,)),
            pltpu.SemaphoreType.DMA((STRIPES,)),
            pltpu.SemaphoreType.DMA((STRIPES,)),
            pltpu.SemaphoreType.DMA((3, STRIPES, group)),
            pltpu.SemaphoreType.DMA((3, STRIPES, group)),
            pltpu.SemaphoreType.DMA((3, STRIPES, 2)),
            pltpu.SemaphoreType.DMA((3, STRIPES, 2)),
            pltpu.SemaphoreType.DMA((bits, STRIPES, group)),
            pltpu.SemaphoreType.DMA((bits, STRIPES, group)),
        ],
        compiler_params=pltpu.CompilerParams(
            collective_id=0, has_side_effects=True, vmem_limit_bytes=grant
        ),
    )(*[pltpu.with_memory_space_constraint(x, pltpu.HBM) for x in tables + arrays])
    pieces = 4
    results = [pltpu.with_memory_space_constraint(x, pltpu.VMEM) for x in (smoothed, coarse)]
    smoothed, coarse = pl.pallas_call(
        functools.partial(deliver, pieces),
        out_shape=tuple(jax.ShapeDtypeStruct(x.shape, x.dtype) for x in (smoothed, coarse)),
        in_specs=[pl.BlockSpec(memory_space=pltpu.VMEM)] * 2,
        out_specs=(anywhere, anywhere),
        scratch_shapes=[pltpu.SemaphoreType.DMA((2, pieces))],
    )(*results)
    return smoothed.reshape(tentative.shape), coarse


def solution(mesh):
    placed = (
        P(("gx", "gy"), None, None, None),
        P(("gx", "gy"), None),
        P(("gx", "gy"), None),
        P(("gx", "gy"), None, None),
        P(("gx", "gy"), None, None, None),
        P(("gx", "gy"), None, None),
        P(("gx", "gy"), None),
        P(("gx", "gy"), None),
        P(("gx", "gy"), None, None),
    )
    return jax.shard_map(
        body,
        mesh=mesh,
        in_specs=placed,
        out_specs=(P(("gx", "gy"), None, None, None), P(("gx", "gy"), None, None)),
        check_vma=False,
    )
```

```python
import functools
import math

import jax
import jax.numpy as jnp
from jax import lax
from jax.experimental import pallas as pl
from jax.experimental.pallas import tpu as pltpu
from jax.sharding import PartitionSpec as P

MESH = pl.DeviceIdType.MESH
STRIPES = 2


def side_by_side(parts):
    return parts[0] if len(parts) == 1 else jnp.concatenate(parts, axis=1)


def kernel(
    dims,
    local_hbm,
    remote_hbm,
    match_hbm,
    peer_hbm,
    slab_hbm,
    slots_hbm,
    operator_hbm,
    tentative_hbm,
    diagonal_hbm,
    smooth_hbm,
    coarse_ref,
    operator,
    diagonal,
    send,
    local_sum,
    turned,
    partial,
    outgoing,
    total,
    local_ref,
    remote_ref,
    match_ref,
    peer_ref,
    slab_ref,
    slots_ref,
    table,
    inverse,
    *rest,
):
    slabs, group, rows, kl, ko, kp, peers, halo, owned = dims
    bits = group.bit_length() - 1
    owns, rest = rest[:STRIPES], rest[STRIPES:]
    rems, rest = (rest[:STRIPES], rest[STRIPES : 2 * STRIPES]), rest[2 * STRIPES :]
    landed = rest[:bits]
    (
        index_sem,
        load_sem,
        rows_sem,
        out_sem,
        send_sem,
        recv_sem,
        slab_send_sem,
        slab_recv_sem,
        half_send_sem,
        half_recv_sem,
    ) = rest[bits:]
    width = operator.shape[-1]
    columns = width // STRIPES
    gx = lax.axis_index("gx")
    me = lax.axis_index("gy")
    has_below = gx > 0
    has_above = gx < slabs - 1
    own_zero = rows * kp
    rem_zero = (group * peers + 2 * halo) * kp
    count = rows * kp * kp
    span = peers * kp
    slab_span = halo * kp
    slab_at = group * span

    def load_rows(s):
        return pltpu.make_async_copy(
            tentative_hbm.at[:, :, pl.ds(s * columns, columns)],
            owns[s].at[pl.ds(0, own_zero)],
            rows_sem.at[s],
        )

    load_peers = pltpu.make_async_copy(peer_hbm, peer_ref, index_sem.at[0])
    load_slabs = pltpu.make_async_copy(slab_hbm, slab_ref, index_sem.at[1])
    load_matches = pltpu.make_async_copy(match_hbm, match_ref, index_sem.at[2])
    load_locals = pltpu.make_async_copy(local_hbm, local_ref, index_sem.at[3])
    load_remotes = pltpu.make_async_copy(remote_hbm, remote_ref, index_sem.at[4])
    load_slots = pltpu.make_async_copy(slots_hbm, slots_ref, index_sem.at[5])
    load_rows(0).start()
    load_peers.start()
    load_slabs.start()

    barrier = pltpu.get_barrier_semaphore()

    def greet(offset, carry):
        pl.semaphore_signal(
            barrier, inc=1, device_id=(gx, (me + offset) % group), device_id_type=MESH
        )
        return carry

    lax.fori_loop(1, group, greet, 0)

    @pl.when(has_below)
    def _():
        pl.semaphore_signal(barrier, inc=1, device_id=(gx - 1, me), device_id_type=MESH)

    @pl.when(has_above)
    def _():
        pl.semaphore_signal(barrier, inc=1, device_id=(gx + 1, me), device_id_type=MESH)

    for s in range(1, STRIPES):
        load_rows(s).start()
    for load in (load_matches, load_locals, load_remotes, load_slots):
        load.start()
    load_operator = pltpu.make_async_copy(operator_hbm, operator, load_sem.at[0])
    load_operator.start()
    load_diagonal = pltpu.make_async_copy(diagonal_hbm, diagonal, load_sem.at[1])
    load_diagonal.start()
    neighbours = jnp.where(has_below, 1, 0) + jnp.where(has_above, 1, 0)
    pl.semaphore_wait(barrier, group - 1 + neighbours)

    def peer_copy(step, s, offset):
        return pltpu.make_async_remote_copy(
            src_ref=send.at[s, pl.ds(offset * span, span)],
            dst_ref=rems[step % 2][s].at[pl.ds(me * span, span)],
            send_sem=send_sem.at[step, s, offset],
            recv_sem=recv_sem.at[step, s, offset],
            device_id=(gx, (me + offset) % group),
            device_id_type=MESH,
        )

    def slab_copy(step, s, way):
        at = slab_at + way * slab_span
        return pltpu.make_async_remote_copy(
            src_ref=send.at[s, pl.ds(at, slab_span)],
            dst_ref=rems[step % 2][s].at[pl.ds(at, slab_span)],
            send_sem=slab_send_sem.at[step, s, way],
            recv_sem=slab_recv_sem.at[step, s, way],
            device_id=(gx + 1 - 2 * way, me),
            device_id_type=MESH,
        )

    def post_rows(step, s):
        def post(turn, carry):
            offset = 1 + turn
            target = (me + offset) % group
            for p in range(peers):
                row = peer_ref[0, target * peers + p]
                for n in range(kp):
                    send[s, offset * span + p * kp + n] = owns[s][row * kp + n]
            peer_copy(step, s, offset).start()
            return carry

        lax.fori_loop(0, group - 1, post, 0)
        for way, present in enumerate((has_above, has_below)):

            @pl.when(present)
            def _():
                for h in range(halo):
                    row = slab_ref[0, way * halo + h]
                    for n in range(kp):
                        send[s, slab_at + way * slab_span + h * kp + n] = owns[s][row * kp + n]
                slab_copy(step, s, way).start()

        for p in range(peers):
            row = peer_ref[0, me * peers + p]
            for n in range(kp):
                rems[step % 2][s][me * span + p * kp + n] = owns[s][row * kp + n]

    def arrive(step, s):
        def finish(turn, carry):
            peer_copy(step, s, 1 + turn).wait()
            return carry

        lax.fori_loop(0, group - 1, finish, 0)
        for way, (sends, receives) in enumerate(((has_above, has_below), (has_below, has_above))):

            @pl.when(sends)
            def _():
                slab_copy(step, s, way).wait_send()

            @pl.when(receives)
            def _():
                slab_copy(step, s, way).wait_recv()

    def tabulate(row, carry):
        for k in range(kl):
            for n in range(kp):
                match = match_ref[k, n, row]
                table[k, n, row] = jnp.where(
                    match == kp, own_zero, local_ref[k, row] * kp + match
                )
        for k in range(ko):
            source = jnp.maximum(remote_ref[k, row] - rows, 0)
            from_below = (source >= group * peers) & (source < group * peers + halo)
            from_above = source >= group * peers + halo
            missing = (from_below & (gx == 0)) | (from_above & (gx == slabs - 1))
            for n in range(kp):
                match = match_ref[kl + k, n, row]
                table[kl + k, n, row] = jnp.where(
                    (match == kp) | missing, rem_zero, source * kp + match
                )
        return carry

    def product(row, first, last, rows_of):
        blocks = [operator[row, k] for k in range(first, last)]
        picked = [
            side_by_side([rows_of[table[k, n, row]] for n in range(kp)])
            for k in range(first, last)
        ]
        return jnp.dot(
            jnp.concatenate(blocks, axis=1),
            jnp.concatenate(picked, axis=0),
            preferred_element_type=jnp.float32,
        )

    def local_rows(s):
        def local_row(row, carry):
            local_sum[s, row] = product(row, 0, kl, owns[s])
            return carry

        lax.fori_loop(0, rows, local_row, 0)

    def image_of(row, step, s):
        value = local_sum[s, row] + product(row, kl, kl + ko, rems[step % 2][s])
        return value.astype(jnp.bfloat16)

    def smooth_rows(step, s):
        def smooth_row(row, carry):
            update = jnp.dot(
                diagonal[row], image_of(row, step, s), preferred_element_type=jnp.float32
            )
            for n in range(kp):
                before = owns[s][row * kp + n].astype(jnp.float32)
                after = before - update[:, n * columns : (n + 1) * columns]
                owns[s][row * kp + n] = after.astype(jnp.bfloat16)
            return carry

        lax.fori_loop(0, rows, smooth_row, 0)

    def turn_row(row, carry):
        for n in range(kp):
            for s in range(STRIPES):
                turned[row, pl.ds(n * width + s * columns, columns)] = owns[s][row * kp + n].T
        return carry

    def partial_rows(step, s):
        def partial_row(row, carry):
            image = image_of(row, step, s)
            stack = jnp.dot(turned[row], image, preferred_element_type=jnp.float32)
            for n in range(kp):
                blocks = stack[n * width : (n + 1) * width].astype(jnp.bfloat16)
                for m in range(kp):
                    at = (row * kp + n) * kp + m
                    partial[s, at] = blocks[:, m * columns : (m + 1) * columns]
            return carry

        lax.fori_loop(0, rows, partial_row, 0)

    core = me % 2
    half = group * owned // 2
    grain = owned

    def invert(at, carry):
        place = at // owned
        high = place // (group // 2)
        odd = (high + me) % 2
        other = high
        for step in range(1, bits):
            bit = (place >> (bits - 1 - step)) & 1
            other = other | jnp.where(odd == 0, bit << step, bit << (bits - step))
        slot = (me ^ other) * owned + at % owned
        found = count
        for row in range(rows):
            for n in range(kp):
                for m in range(kp):
                    named = (row * kp + n) * kp + m
                    found = jnp.where(slots_ref[n, m, row] == slot, named, found)
        inverse[at] = found
        return carry

    def partner(step):
        def flip(bit):
            return me + bit * (1 - 2 * ((me // bit) % 2))

        if step == 0:
            return flip(1)
        return (1 - core) * flip(1 << step) + core * flip(1 << (bits - step))

    def half_copy(step, s, chunk):
        at = chunk * grain
        if step == 0:
            source = outgoing.at[s, pl.ds(at, grain)]
        else:
            source = total.at[s, pl.ds((half >> step) + at, grain)]
        return pltpu.make_async_remote_copy(
            src_ref=source,
            dst_ref=landed[step].at[s, pl.ds(at, grain)],
            send_sem=half_send_sem.at[step, s, chunk],
            recv_sem=half_recv_sem.at[step, s, chunk],
            device_id=(gx, partner(step)),
            device_id_type=MESH,
        )

    def send_partials(s):
        def send_chunk(turn, carry):
            chunk = half // grain - 1 - turn
            for j in range(grain):
                at = chunk * grain + j
                outgoing[s, at] = partial[s, inverse[half + at]]
            half_copy(0, s, chunk).start()
            return carry

        lax.fori_loop(0, half // grain, send_chunk, 0)

    def add_partials(step, s):
        last = step == bits - 1
        chunks = (half >> step) // grain

        def add(chunk):
            half_copy(step, s, chunk).wait_recv()
            for j in range(grain):
                at = chunk * grain + j
                mine = partial[s, inverse[at]] if step == 0 else total[s, at]
                value = mine.astype(jnp.float32) + landed[step][s, at].astype(jnp.float32)
                if last:
                    coarse_ref[at, :, s * columns : (s + 1) * columns] = value.astype(jnp.bfloat16)
                else:
                    total[s, at] = value.astype(jnp.bfloat16)

        if last:
            for chunk in reversed(range(chunks)):
                add(chunk)
            return

        def upper(turn, carry):
            chunk = chunks - 1 - turn
            add(chunk)
            half_copy(step + 1, s, chunk - chunks // 2).start()
            return carry

        def lower(turn, carry):
            add(chunks // 2 - 1 - turn)
            return carry

        lax.fori_loop(0, chunks // 2, upper, 0)
        lax.fori_loop(0, chunks // 2, lower, 0)

    stripes = range(STRIPES)
    load_peers.wait()
    load_slabs.wait()
    load_rows(0).wait()
    post_rows(0, 0)
    zero = jnp.zeros((width, columns), jnp.bfloat16)
    for s in range(STRIPES):
        owns[s][own_zero] = zero
        for rem in rems:
            rem[s][rem_zero] = zero
        partial[s, count] = zero
    load_matches.wait()
    load_locals.wait()
    load_remotes.wait()
    lax.fori_loop(0, rows, tabulate, 0)
    for s in stripes[1:]:
        load_rows(s).wait()
    load_operator.wait()
    for s in stripes:
        local_rows(s)
    for s in stripes[1:]:
        post_rows(0, s)
    load_slots.wait()
    lax.fori_loop(0, group * owned, invert, 0)
    load_diagonal.wait()

    stores = []
    for step in range(2):
        for s in stripes:
            arrive(step, s)
            smooth_rows(step, s)
            if s == STRIPES - 1:
                local_rows(s)
                if step == 1:
                    lax.fori_loop(0, rows, turn_row, 0)
            post_rows(step + 1, s)
            if step == 1:
                store = pltpu.make_async_copy(
                    owns[s].at[pl.ds(0, own_zero)],
                    smooth_hbm.at[:, :, pl.ds(s * columns, columns)],
                    out_sem.at[s],
                )
                store.start()
                stores.append(store)
            if s < STRIPES - 1:
                local_rows(s)

    for s in stripes:
        if s > 0:
            add_partials(0, s - 1)
        arrive(2, s)
        partial_rows(2, s)
        send_partials(s)
    for step in range(1, bits):
        add_partials(step, 0)
        add_partials(step - 1, 1)
    add_partials(bits - 1, 1)
    for s in stripes:
        for step in range(bits):
            for chunk in range((half >> step) // grain):
                half_copy(step, s, chunk).wait_send()
    for store in stores:
        store.wait()


def deliver(pieces, smooth_ref, coarse_ref, smooth_out, coarse_out, sem):
    copies = []
    for which, (source, target) in enumerate(((smooth_ref, smooth_out), (coarse_ref, coarse_out))):
        step = pl.cdiv(source.shape[0], pieces)
        for piece, at in enumerate(range(0, source.shape[0], step)):
            window = pl.ds(at, min(step, source.shape[0] - at))
            copies.append(
                pltpu.make_async_copy(
                    source.at[window], target.at[window], sem.at[which, piece]
                )
            )
    for copy in copies:
        copy.start()
    for copy in copies:
        copy.wait()


def body(
    operator_blocks,
    local_columns,
    remote_columns,
    match_slots,
    tentative,
    inverse_diagonal,
    peer_sends,
    slab_sends,
    coarse_slots,
):
    slabs = lax.axis_size("gx")
    group = lax.axis_size("gy")
    rows, kp, width = tentative.shape[:3]
    kl, ko = local_columns.shape[1], remote_columns.shape[1]
    peers = peer_sends.shape[1] // group
    halo = slab_sends.shape[1] // 2
    owned = (3 * rows * kp * kp // 2 + group - 1) // group
    bits = group.bit_length() - 1
    count = rows * kp * kp
    columns = width // STRIPES
    dims = (slabs, group, rows, kl, ko, kp, peers, halo, owned)

    def blocks(n):
        return pltpu.VMEM((STRIPES, n, width, columns), jnp.bfloat16)

    tables = (
        local_columns.T,
        remote_columns.T,
        match_slots.transpose(1, 2, 0),
        peer_sends,
        slab_sends,
        coarse_slots.transpose(1, 2, 0),
    )
    arrays = (operator_blocks, tentative.reshape(rows * kp, width, width), inverse_diagonal)
    anywhere = pl.BlockSpec(memory_space=pl.ANY)
    half = group * owned // 2
    remote_count = (group * peers + 2 * halo) * kp
    vmem = [
        pltpu.VMEM(operator_blocks.shape, jnp.bfloat16),
        pltpu.VMEM((rows, width, width), jnp.bfloat16),
        blocks(remote_count),
        pltpu.VMEM((STRIPES, rows, width, kp * columns), jnp.float32),
        pltpu.VMEM((rows, kp * width, width), jnp.bfloat16),
        blocks(count + 1),
        blocks(half),
        blocks(half),
    ]
    striped = [pltpu.VMEM((rows * kp + 1, width, columns), jnp.bfloat16)] * STRIPES
    striped += [pltpu.VMEM((remote_count + 1, width, columns), jnp.bfloat16)] * (2 * STRIPES)
    landed = [blocks(half >> step) for step in range(bits)]
    used = sum(
        math.prod(x.shape) * jnp.dtype(x.dtype).itemsize for x in [*vmem, *striped, *landed]
    )
    grant = used + owned * width * width * 2 + (1 << 20)
    smoothed, coarse = pl.pallas_call(
        functools.partial(kernel, dims),
        out_shape=(
            jax.ShapeDtypeStruct((rows * kp, width, width), jnp.bfloat16),
            jax.ShapeDtypeStruct((owned, width, width), jnp.bfloat16),
        ),
        in_specs=[pl.BlockSpec(memory_space=pltpu.HBM)] * 9,
        out_specs=(anywhere, pl.BlockSpec(memory_space=pltpu.VMEM)),
        scratch_shapes=[
            *vmem,
            *[pltpu.SMEM(table.shape, jnp.int32) for table in tables],
            pltpu.SMEM((kl + ko, kp, rows), jnp.int32),
            pltpu.SMEM((2 * half,), jnp.int32),
            *striped,
            *landed,
            pltpu.SemaphoreType.DMA((len(tables),)),
            pltpu.SemaphoreType.DMA((2,)),
            pltpu.SemaphoreType.DMA((STRIPES,)),
            pltpu.SemaphoreType.DMA((STRIPES,)),
            pltpu.SemaphoreType.DMA((3, STRIPES, group)),
            pltpu.SemaphoreType.DMA((3, STRIPES, group)),
            pltpu.SemaphoreType.DMA((3, STRIPES, 2)),
            pltpu.SemaphoreType.DMA((3, STRIPES, 2)),
            pltpu.SemaphoreType.DMA((bits, STRIPES, group)),
            pltpu.SemaphoreType.DMA((bits, STRIPES, group)),
        ],
        compiler_params=pltpu.CompilerParams(
            collective_id=0, has_side_effects=True, vmem_limit_bytes=grant
        ),
    )(*[pltpu.with_memory_space_constraint(x, pltpu.HBM) for x in tables + arrays])
    pieces = 4
    results = [pltpu.with_memory_space_constraint(x, pltpu.VMEM) for x in (smoothed, coarse)]
    smoothed, coarse = pl.pallas_call(
        functools.partial(deliver, pieces),
        out_shape=tuple(jax.ShapeDtypeStruct(x.shape, x.dtype) for x in (smoothed, coarse)),
        in_specs=[pl.BlockSpec(memory_space=pltpu.VMEM)] * 2,
        out_specs=(anywhere, anywhere),
        scratch_shapes=[pltpu.SemaphoreType.DMA((2, pieces))],
    )(*results)
    return smoothed.reshape(tentative.shape), coarse


def solution(mesh):
    placed = (
        P(("gx", "gy"), None, None, None),
        P(("gx", "gy"), None),
        P(("gx", "gy"), None),
        P(("gx", "gy"), None, None),
        P(("gx", "gy"), None, None, None),
        P(("gx", "gy"), None, None),
        P(("gx", "gy"), None),
        P(("gx", "gy"), None),
        P(("gx", "gy"), None, None),
    )
    return jax.shard_map(
        body,
        mesh=mesh,
        in_specs=placed,
        out_specs=(P(("gx", "gy"), None, None, None), P(("gx", "gy"), None, None)),
        check_vma=False,
    )
```

```python
import functools
import math

import jax
import jax.numpy as jnp
from jax import lax
from jax.experimental import pallas as pl
from jax.experimental.pallas import tpu as pltpu
from jax.sharding import PartitionSpec as P

MESH = pl.DeviceIdType.MESH
STRIPES = 2


def side_by_side(parts):
    return parts[0] if len(parts) == 1 else jnp.concatenate(parts, axis=1)


def kernel(
    dims,
    local_hbm,
    remote_hbm,
    match_hbm,
    peer_hbm,
    slab_hbm,
    slots_hbm,
    operator_hbm,
    tentative_hbm,
    diagonal_hbm,
    smooth_hbm,
    coarse_ref,
    operator,
    diagonal,
    send,
    local_sum,
    turned,
    partial,
    outgoing,
    total,
    local_ref,
    remote_ref,
    match_ref,
    peer_ref,
    slab_ref,
    slots_ref,
    table,
    inverse,
    *rest,
):
    slabs, group, rows, kl, ko, kp, peers, halo, owned = dims
    bits = group.bit_length() - 1
    owns, rest = rest[:STRIPES], rest[STRIPES:]
    rems, rest = (rest[:STRIPES], rest[STRIPES : 2 * STRIPES]), rest[2 * STRIPES :]
    landed = rest[:bits]
    (
        index_sem,
        load_sem,
        rows_sem,
        out_sem,
        send_sem,
        recv_sem,
        slab_send_sem,
        slab_recv_sem,
        half_send_sem,
        half_recv_sem,
    ) = rest[bits:]
    width = operator.shape[-1]
    columns = width // STRIPES
    gx = lax.axis_index("gx")
    me = lax.axis_index("gy")
    has_below = gx > 0
    has_above = gx < slabs - 1
    own_zero = rows * kp
    rem_zero = (group * peers + 2 * halo) * kp
    count = rows * kp * kp
    span = peers * kp
    slab_span = halo * kp
    slab_at = group * span

    def load_rows(s):
        return pltpu.make_async_copy(
            tentative_hbm.at[:, :, pl.ds(s * columns, columns)],
            owns[s].at[pl.ds(0, own_zero)],
            rows_sem.at[s],
        )

    load_peers = pltpu.make_async_copy(peer_hbm, peer_ref, index_sem.at[0])
    load_slabs = pltpu.make_async_copy(slab_hbm, slab_ref, index_sem.at[1])
    load_matches = pltpu.make_async_copy(match_hbm, match_ref, index_sem.at[2])
    load_locals = pltpu.make_async_copy(local_hbm, local_ref, index_sem.at[3])
    load_remotes = pltpu.make_async_copy(remote_hbm, remote_ref, index_sem.at[4])
    load_slots = pltpu.make_async_copy(slots_hbm, slots_ref, index_sem.at[5])
    load_rows(0).start()
    load_peers.start()
    load_slabs.start()

    barrier = pltpu.get_barrier_semaphore()

    def greet(offset, carry):
        pl.semaphore_signal(
            barrier, inc=1, device_id=(gx, (me + offset) % group), device_id_type=MESH
        )
        return carry

    lax.fori_loop(1, group, greet, 0)

    @pl.when(has_below)
    def _():
        pl.semaphore_signal(barrier, inc=1, device_id=(gx - 1, me), device_id_type=MESH)

    @pl.when(has_above)
    def _():
        pl.semaphore_signal(barrier, inc=1, device_id=(gx + 1, me), device_id_type=MESH)

    for s in range(1, STRIPES):
        load_rows(s).start()
    for load in (load_matches, load_locals, load_remotes, load_slots):
        load.start()
    load_operator = pltpu.make_async_copy(operator_hbm, operator, load_sem.at[0])
    load_operator.start()
    load_diagonal = pltpu.make_async_copy(diagonal_hbm, diagonal, load_sem.at[1])
    load_diagonal.start()
    neighbours = jnp.where(has_below, 1, 0) + jnp.where(has_above, 1, 0)
    pl.semaphore_wait(barrier, group - 1 + neighbours)

    def peer_copy(step, s, offset):
        return pltpu.make_async_remote_copy(
            src_ref=send.at[s, pl.ds(offset * span, span)],
            dst_ref=rems[step % 2][s].at[pl.ds(me * span, span)],
            send_sem=send_sem.at[step, s, offset],
            recv_sem=recv_sem.at[step, s, offset],
            device_id=(gx, (me + offset) % group),
            device_id_type=MESH,
        )

    def slab_copy(step, s, way):
        at = slab_at + way * slab_span
        return pltpu.make_async_remote_copy(
            src_ref=send.at[s, pl.ds(at, slab_span)],
            dst_ref=rems[step % 2][s].at[pl.ds(at, slab_span)],
            send_sem=slab_send_sem.at[step, s, way],
            recv_sem=slab_recv_sem.at[step, s, way],
            device_id=(gx + 1 - 2 * way, me),
            device_id_type=MESH,
        )

    def post_rows(step, s):
        def post(turn, carry):
            offset = 1 + turn
            target = (me + offset) % group
            for p in range(peers):
                row = peer_ref[0, target * peers + p]
                for n in range(kp):
                    send[s, offset * span + p * kp + n] = owns[s][row * kp + n]
            peer_copy(step, s, offset).start()
            return carry

        for way, present in enumerate((has_above, has_below)):

            @pl.when(present)
            def _():
                for h in range(halo):
                    row = slab_ref[0, way * halo + h]
                    for n in range(kp):
                        send[s, slab_at + way * slab_span + h * kp + n] = owns[s][row * kp + n]
                slab_copy(step, s, way).start()

        lax.fori_loop(0, group - 1, post, 0)
        for p in range(peers):
            row = peer_ref[0, me * peers + p]
            for n in range(kp):
                rems[step % 2][s][me * span + p * kp + n] = owns[s][row * kp + n]

    def arrive(step, s):
        def finish(turn, carry):
            peer_copy(step, s, 1 + turn).wait()
            return carry

        lax.fori_loop(0, group - 1, finish, 0)
        for way, (sends, receives) in enumerate(((has_above, has_below), (has_below, has_above))):

            @pl.when(sends)
            def _():
                slab_copy(step, s, way).wait_send()

            @pl.when(receives)
            def _():
                slab_copy(step, s, way).wait_recv()

    def tabulate(row, carry):
        for k in range(kl):
            for n in range(kp):
                match = match_ref[k, n, row]
                table[k, n, row] = jnp.where(
                    match == kp, own_zero, local_ref[k, row] * kp + match
                )
        for k in range(ko):
            source = jnp.maximum(remote_ref[k, row] - rows, 0)
            from_below = (source >= group * peers) & (source < group * peers + halo)
            from_above = source >= group * peers + halo
            missing = (from_below & (gx == 0)) | (from_above & (gx == slabs - 1))
            for n in range(kp):
                match = match_ref[kl + k, n, row]
                table[kl + k, n, row] = jnp.where(
                    (match == kp) | missing, rem_zero, source * kp + match
                )
        return carry

    def product(row, first, last, rows_of):
        blocks = [operator[row, k] for k in range(first, last)]
        picked = [
            side_by_side([rows_of[table[k, n, row]] for n in range(kp)])
            for k in range(first, last)
        ]
        return jnp.dot(
            jnp.concatenate(blocks, axis=1),
            jnp.concatenate(picked, axis=0),
            preferred_element_type=jnp.float32,
        )

    def local_rows(s):
        def local_row(row, carry):
            local_sum[s, row] = product(row, 0, kl, owns[s])
            return carry

        lax.fori_loop(0, rows, local_row, 0)

    def image_of(row, step, s):
        value = local_sum[s, row] + product(row, kl, kl + ko, rems[step % 2][s])
        return value.astype(jnp.bfloat16)

    def smooth_rows(step, s):
        def smooth_row(row, carry):
            update = jnp.dot(
                diagonal[row], image_of(row, step, s), preferred_element_type=jnp.float32
            )
            for n in range(kp):
                before = owns[s][row * kp + n].astype(jnp.float32)
                after = before - update[:, n * columns : (n + 1) * columns]
                owns[s][row * kp + n] = after.astype(jnp.bfloat16)
            return carry

        lax.fori_loop(0, rows, smooth_row, 0)

    def turn_row(row, carry):
        for n in range(kp):
            for s in range(STRIPES):
                turned[row, pl.ds(n * width + s * columns, columns)] = owns[s][row * kp + n].T
        return carry

    def partial_rows(step, s):
        def partial_row(row, carry):
            image = image_of(row, step, s)
            stack = jnp.dot(turned[row], image, preferred_element_type=jnp.float32)
            for n in range(kp):
                blocks = stack[n * width : (n + 1) * width].astype(jnp.bfloat16)
                for m in range(kp):
                    at = (row * kp + n) * kp + m
                    partial[s, at] = blocks[:, m * columns : (m + 1) * columns]
            return carry

        lax.fori_loop(0, rows, partial_row, 0)

    core = me % 2
    half = group * owned // 2
    grain = owned

    def invert(at, carry):
        place = at // owned
        high = place // (group // 2)
        odd = (high + me) % 2
        other = high
        for step in range(1, bits):
            bit = (place >> (bits - 1 - step)) & 1
            other = other | jnp.where(odd == 0, bit << step, bit << (bits - step))
        slot = (me ^ other) * owned + at % owned
        found = count
        for row in range(rows):
            for n in range(kp):
                for m in range(kp):
                    named = (row * kp + n) * kp + m
                    found = jnp.where(slots_ref[n, m, row] == slot, named, found)
        inverse[at] = found
        return carry

    def partner(step):
        def flip(bit):
            return me + bit * (1 - 2 * ((me // bit) % 2))

        if step == 0:
            return flip(1)
        return (1 - core) * flip(1 << step) + core * flip(1 << (bits - step))

    def half_copy(step, s, chunk):
        at = chunk * grain
        if step == 0:
            source = outgoing.at[s, pl.ds(at, grain)]
        else:
            source = total.at[s, pl.ds((half >> step) + at, grain)]
        return pltpu.make_async_remote_copy(
            src_ref=source,
            dst_ref=landed[step].at[s, pl.ds(at, grain)],
            send_sem=half_send_sem.at[step, s, chunk],
            recv_sem=half_recv_sem.at[step, s, chunk],
            device_id=(gx, partner(step)),
            device_id_type=MESH,
        )

    def send_partials(s):
        def send_chunk(turn, carry):
            chunk = half // grain - 1 - turn
            for j in range(grain):
                at = chunk * grain + j
                outgoing[s, at] = partial[s, inverse[half + at]]
            half_copy(0, s, chunk).start()
            return carry

        lax.fori_loop(0, half // grain, send_chunk, 0)

    def add_partials(step, s):
        last = step == bits - 1
        chunks = (half >> step) // grain

        def add(chunk):
            half_copy(step, s, chunk).wait_recv()
            for j in range(grain):
                at = chunk * grain + j
                mine = partial[s, inverse[at]] if step == 0 else total[s, at]
                value = mine.astype(jnp.float32) + landed[step][s, at].astype(jnp.float32)
                if last:
                    coarse_ref[at, :, s * columns : (s + 1) * columns] = value.astype(jnp.bfloat16)
                else:
                    total[s, at] = value.astype(jnp.bfloat16)

        if last:
            for chunk in reversed(range(chunks)):
                add(chunk)
            return

        def upper(turn, carry):
            chunk = chunks - 1 - turn
            add(chunk)
            half_copy(step + 1, s, chunk - chunks // 2).start()
            return carry

        def lower(turn, carry):
            add(chunks // 2 - 1 - turn)
            return carry

        lax.fori_loop(0, chunks // 2, upper, 0)
        lax.fori_loop(0, chunks // 2, lower, 0)

    stripes = range(STRIPES)
    load_peers.wait()
    load_slabs.wait()
    load_rows(0).wait()
    post_rows(0, 0)
    zero = jnp.zeros((width, columns), jnp.bfloat16)
    for s in range(STRIPES):
        owns[s][own_zero] = zero
        for rem in rems:
            rem[s][rem_zero] = zero
        partial[s, count] = zero
    load_matches.wait()
    load_locals.wait()
    load_remotes.wait()
    lax.fori_loop(0, rows, tabulate, 0)
    for s in stripes[1:]:
        load_rows(s).wait()
    load_operator.wait()
    local_rows(0)
    for s in stripes[1:]:
        post_rows(0, s)
        local_rows(s)
    load_slots.wait()
    lax.fori_loop(0, group * owned, invert, 0)
    load_diagonal.wait()

    stores = []
    for step in range(2):
        for s in stripes:
            arrive(step, s)
            smooth_rows(step, s)
            if s == STRIPES - 1:
                local_rows(s)
                if step == 1:
                    lax.fori_loop(0, rows, turn_row, 0)
            post_rows(step + 1, s)
            if step == 1:
                store = pltpu.make_async_copy(
                    owns[s].at[pl.ds(0, own_zero)],
                    smooth_hbm.at[:, :, pl.ds(s * columns, columns)],
                    out_sem.at[s],
                )
                store.start()
                stores.append(store)
            if s < STRIPES - 1:
                local_rows(s)

    for s in stripes:
        if s > 0:
            add_partials(0, s - 1)
        arrive(2, s)
        partial_rows(2, s)
        send_partials(s)
    for step in range(1, bits):
        add_partials(step, 0)
        add_partials(step - 1, 1)
    add_partials(bits - 1, 1)
    for s in stripes:
        for step in range(bits):
            for chunk in range((half >> step) // grain):
                half_copy(step, s, chunk).wait_send()
    for store in stores:
        store.wait()


def deliver(pieces, smooth_ref, coarse_ref, smooth_out, coarse_out, sem):
    copies = []
    for which, (source, target) in enumerate(((smooth_ref, smooth_out), (coarse_ref, coarse_out))):
        step = pl.cdiv(source.shape[0], pieces)
        for piece, at in enumerate(range(0, source.shape[0], step)):
            window = pl.ds(at, min(step, source.shape[0] - at))
            copies.append(
                pltpu.make_async_copy(
                    source.at[window], target.at[window], sem.at[which, piece]
                )
            )
    for copy in copies:
        copy.start()
    for copy in copies:
        copy.wait()


def body(
    operator_blocks,
    local_columns,
    remote_columns,
    match_slots,
    tentative,
    inverse_diagonal,
    peer_sends,
    slab_sends,
    coarse_slots,
):
    slabs = lax.axis_size("gx")
    group = lax.axis_size("gy")
    rows, kp, width = tentative.shape[:3]
    kl, ko = local_columns.shape[1], remote_columns.shape[1]
    peers = peer_sends.shape[1] // group
    halo = slab_sends.shape[1] // 2
    owned = (3 * rows * kp * kp // 2 + group - 1) // group
    bits = group.bit_length() - 1
    count = rows * kp * kp
    columns = width // STRIPES
    dims = (slabs, group, rows, kl, ko, kp, peers, halo, owned)

    def blocks(n):
        return pltpu.VMEM((STRIPES, n, width, columns), jnp.bfloat16)

    tables = (
        local_columns.T,
        remote_columns.T,
        match_slots.transpose(1, 2, 0),
        peer_sends,
        slab_sends,
        coarse_slots.transpose(1, 2, 0),
    )
    arrays = (operator_blocks, tentative.reshape(rows * kp, width, width), inverse_diagonal)
    anywhere = pl.BlockSpec(memory_space=pl.ANY)
    half = group * owned // 2
    remote_count = (group * peers + 2 * halo) * kp
    vmem = [
        pltpu.VMEM(operator_blocks.shape, jnp.bfloat16),
        pltpu.VMEM((rows, width, width), jnp.bfloat16),
        blocks(remote_count),
        pltpu.VMEM((STRIPES, rows, width, kp * columns), jnp.float32),
        pltpu.VMEM((rows, kp * width, width), jnp.bfloat16),
        blocks(count + 1),
        blocks(half),
        blocks(half),
    ]
    striped = [pltpu.VMEM((rows * kp + 1, width, columns), jnp.bfloat16)] * STRIPES
    striped += [pltpu.VMEM((remote_count + 1, width, columns), jnp.bfloat16)] * (2 * STRIPES)
    landed = [blocks(half >> step) for step in range(bits)]
    used = sum(
        math.prod(x.shape) * jnp.dtype(x.dtype).itemsize for x in [*vmem, *striped, *landed]
    )
    grant = used + owned * width * width * 2 + (1 << 20)
    smoothed, coarse = pl.pallas_call(
        functools.partial(kernel, dims),
        out_shape=(
            jax.ShapeDtypeStruct((rows * kp, width, width), jnp.bfloat16),
            jax.ShapeDtypeStruct((owned, width, width), jnp.bfloat16),
        ),
        in_specs=[pl.BlockSpec(memory_space=pltpu.HBM)] * 9,
        out_specs=(anywhere, pl.BlockSpec(memory_space=pltpu.VMEM)),
        scratch_shapes=[
            *vmem,
            *[pltpu.SMEM(table.shape, jnp.int32) for table in tables],
            pltpu.SMEM((kl + ko, kp, rows), jnp.int32),
            pltpu.SMEM((2 * half,), jnp.int32),
            *striped,
            *landed,
            pltpu.SemaphoreType.DMA((len(tables),)),
            pltpu.SemaphoreType.DMA((2,)),
            pltpu.SemaphoreType.DMA((STRIPES,)),
            pltpu.SemaphoreType.DMA((STRIPES,)),
            pltpu.SemaphoreType.DMA((3, STRIPES, group)),
            pltpu.SemaphoreType.DMA((3, STRIPES, group)),
            pltpu.SemaphoreType.DMA((3, STRIPES, 2)),
            pltpu.SemaphoreType.DMA((3, STRIPES, 2)),
            pltpu.SemaphoreType.DMA((bits, STRIPES, group)),
            pltpu.SemaphoreType.DMA((bits, STRIPES, group)),
        ],
        compiler_params=pltpu.CompilerParams(
            collective_id=0, has_side_effects=True, vmem_limit_bytes=grant
        ),
    )(*[pltpu.with_memory_space_constraint(x, pltpu.HBM) for x in tables + arrays])
    pieces = 4
    results = [pltpu.with_memory_space_constraint(x, pltpu.VMEM) for x in (smoothed, coarse)]
    smoothed, coarse = pl.pallas_call(
        functools.partial(deliver, pieces),
        out_shape=tuple(jax.ShapeDtypeStruct(x.shape, x.dtype) for x in (smoothed, coarse)),
        in_specs=[pl.BlockSpec(memory_space=pltpu.VMEM)] * 2,
        out_specs=(anywhere, anywhere),
        scratch_shapes=[pltpu.SemaphoreType.DMA((2, pieces))],
    )(*results)
    return smoothed.reshape(tentative.shape), coarse


def solution(mesh):
    placed = (
        P(("gx", "gy"), None, None, None),
        P(("gx", "gy"), None),
        P(("gx", "gy"), None),
        P(("gx", "gy"), None, None),
        P(("gx", "gy"), None, None, None),
        P(("gx", "gy"), None, None),
        P(("gx", "gy"), None),
        P(("gx", "gy"), None),
        P(("gx", "gy"), None, None),
    )
    return jax.shard_map(
        body,
        mesh=mesh,
        in_specs=placed,
        out_specs=(P(("gx", "gy"), None, None, None), P(("gx", "gy"), None, None)),
        check_vma=False,
    )
```

```python
import functools
import math

import jax
import jax.numpy as jnp
from jax import lax
from jax.experimental import pallas as pl
from jax.experimental.pallas import tpu as pltpu
from jax.sharding import PartitionSpec as P

MESH = pl.DeviceIdType.MESH
STRIPES = 2


def side_by_side(parts):
    return parts[0] if len(parts) == 1 else jnp.concatenate(parts, axis=1)


def kernel(
    dims,
    local_hbm,
    remote_hbm,
    match_hbm,
    peer_hbm,
    slab_hbm,
    slots_hbm,
    operator_hbm,
    tentative_hbm,
    diagonal_hbm,
    smooth_hbm,
    coarse_ref,
    operator,
    diagonal,
    send,
    local_sum,
    turned,
    partial,
    outgoing,
    total,
    local_ref,
    remote_ref,
    match_ref,
    peer_ref,
    slab_ref,
    slots_ref,
    table,
    inverse,
    *rest,
):
    slabs, group, rows, kl, ko, kp, peers, halo, owned = dims
    bits = group.bit_length() - 1
    owns, rest = rest[:STRIPES], rest[STRIPES:]
    rems, rest = (rest[:STRIPES], rest[STRIPES : 2 * STRIPES]), rest[2 * STRIPES :]
    landed = rest[:bits]
    (
        index_sem,
        load_sem,
        rows_sem,
        out_sem,
        send_sem,
        recv_sem,
        slab_send_sem,
        slab_recv_sem,
        half_send_sem,
        half_recv_sem,
    ) = rest[bits:]
    width = operator.shape[-1]
    columns = width // STRIPES
    gx = lax.axis_index("gx")
    me = lax.axis_index("gy")
    has_below = gx > 0
    has_above = gx < slabs - 1
    own_zero = rows * kp
    rem_zero = (group * peers + 2 * halo) * kp
    count = rows * kp * kp
    span = peers * kp
    slab_span = halo * kp
    slab_at = group * span

    def load_rows(s):
        return pltpu.make_async_copy(
            tentative_hbm.at[:, :, pl.ds(s * columns, columns)],
            owns[s].at[pl.ds(0, own_zero)],
            rows_sem.at[s],
        )

    load_peers = pltpu.make_async_copy(peer_hbm, peer_ref, index_sem.at[0])
    load_slabs = pltpu.make_async_copy(slab_hbm, slab_ref, index_sem.at[1])
    load_matches = pltpu.make_async_copy(match_hbm, match_ref, index_sem.at[2])
    load_locals = pltpu.make_async_copy(local_hbm, local_ref, index_sem.at[3])
    load_remotes = pltpu.make_async_copy(remote_hbm, remote_ref, index_sem.at[4])
    load_slots = pltpu.make_async_copy(slots_hbm, slots_ref, index_sem.at[5])
    load_rows(0).start()
    load_peers.start()
    load_slabs.start()

    barrier = pltpu.get_barrier_semaphore()

    def greet(offset, carry):
        pl.semaphore_signal(
            barrier, inc=1, device_id=(gx, (me + offset) % group), device_id_type=MESH
        )
        return carry

    lax.fori_loop(1, group, greet, 0)

    @pl.when(has_below)
    def _():
        pl.semaphore_signal(barrier, inc=1, device_id=(gx - 1, me), device_id_type=MESH)

    @pl.when(has_above)
    def _():
        pl.semaphore_signal(barrier, inc=1, device_id=(gx + 1, me), device_id_type=MESH)

    for s in range(1, STRIPES):
        load_rows(s).start()
    for load in (load_matches, load_locals, load_remotes, load_slots):
        load.start()
    load_operator = pltpu.make_async_copy(operator_hbm, operator, load_sem.at[0])
    load_operator.start()
    load_diagonal = pltpu.make_async_copy(diagonal_hbm, diagonal, load_sem.at[1])
    load_diagonal.start()
    neighbours = jnp.where(has_below, 1, 0) + jnp.where(has_above, 1, 0)
    pl.semaphore_wait(barrier, group - 1 + neighbours)

    def peer_copy(step, s, offset):
        return pltpu.make_async_remote_copy(
            src_ref=send.at[s, pl.ds(offset * span, span)],
            dst_ref=rems[step % 2][s].at[pl.ds(me * span, span)],
            send_sem=send_sem.at[step, s, offset],
            recv_sem=recv_sem.at[step, s, offset],
            device_id=(gx, (me + offset) % group),
            device_id_type=MESH,
        )

    def slab_copy(step, s, way):
        at = slab_at + way * slab_span
        return pltpu.make_async_remote_copy(
            src_ref=send.at[s, pl.ds(at, slab_span)],
            dst_ref=rems[step % 2][s].at[pl.ds(at, slab_span)],
            send_sem=slab_send_sem.at[step, s, way],
            recv_sem=slab_recv_sem.at[step, s, way],
            device_id=(gx + 1 - 2 * way, me),
            device_id_type=MESH,
        )

    def post_rows(step, s):
        def post(turn, carry):
            offset = 1 + turn
            target = (me + offset) % group
            for p in range(peers):
                row = peer_ref[0, target * peers + p]
                for n in range(kp):
                    send[s, offset * span + p * kp + n] = owns[s][row * kp + n]
            peer_copy(step, s, offset).start()
            return carry

        lax.fori_loop(0, group - 1, post, 0)
        for way, present in enumerate((has_above, has_below)):

            @pl.when(present)
            def _():
                for h in range(halo):
                    row = slab_ref[0, way * halo + h]
                    for n in range(kp):
                        send[s, slab_at + way * slab_span + h * kp + n] = owns[s][row * kp + n]
                slab_copy(step, s, way).start()

        for p in range(peers):
            row = peer_ref[0, me * peers + p]
            for n in range(kp):
                rems[step % 2][s][me * span + p * kp + n] = owns[s][row * kp + n]

    def arrive(step, s):
        def finish(turn, carry):
            peer_copy(step, s, 1 + turn).wait()
            return carry

        lax.fori_loop(0, group - 1, finish, 0)
        for way, (sends, receives) in enumerate(((has_above, has_below), (has_below, has_above))):

            @pl.when(sends)
            def _():
                slab_copy(step, s, way).wait_send()

            @pl.when(receives)
            def _():
                slab_copy(step, s, way).wait_recv()

    def tabulate(row, carry):
        for k in range(kl):
            for n in range(kp):
                match = match_ref[k, n, row]
                table[k, n, row] = jnp.where(
                    match == kp, own_zero, local_ref[k, row] * kp + match
                )
        for k in range(ko):
            source = jnp.maximum(remote_ref[k, row] - rows, 0)
            from_below = (source >= group * peers) & (source < group * peers + halo)
            from_above = source >= group * peers + halo
            missing = (from_below & (gx == 0)) | (from_above & (gx == slabs - 1))
            for n in range(kp):
                match = match_ref[kl + k, n, row]
                table[kl + k, n, row] = jnp.where(
                    (match == kp) | missing, rem_zero, source * kp + match
                )
        return carry

    def product(row, first, last, rows_of):
        blocks = [operator[row, k] for k in range(first, last)]
        picked = [
            side_by_side([rows_of[table[k, n, row]] for n in range(kp)])
            for k in range(first, last)
        ]
        return jnp.dot(
            jnp.concatenate(blocks, axis=1),
            jnp.concatenate(picked, axis=0),
            preferred_element_type=jnp.float32,
        )

    def local_rows(s):
        def local_row(row, carry):
            local_sum[s, row] = product(row, 0, kl, owns[s])
            return carry

        lax.fori_loop(0, rows, local_row, 0)

    def image_of(row, step, s):
        value = local_sum[s, row] + product(row, kl, kl + ko, rems[step % 2][s])
        return value.astype(jnp.bfloat16)

    def smooth_rows(step, s):
        def smooth_row(row, carry):
            update = jnp.dot(
                diagonal[row], image_of(row, step, s), preferred_element_type=jnp.float32
            )
            for n in range(kp):
                before = owns[s][row * kp + n].astype(jnp.float32)
                after = before - update[:, n * columns : (n + 1) * columns]
                owns[s][row * kp + n] = after.astype(jnp.bfloat16)
            return carry

        lax.fori_loop(0, rows, smooth_row, 0)

    def turn_row(row, carry):
        for n in range(kp):
            for s in range(STRIPES):
                turned[row, pl.ds(n * width + s * columns, columns)] = owns[s][row * kp + n].T
        return carry

    def partial_rows(step, s):
        def partial_row(row, carry):
            image = image_of(row, step, s)
            stack = jnp.dot(turned[row], image, preferred_element_type=jnp.float32)
            for n in range(kp):
                blocks = stack[n * width : (n + 1) * width].astype(jnp.bfloat16)
                for m in range(kp):
                    at = (row * kp + n) * kp + m
                    partial[s, at] = blocks[:, m * columns : (m + 1) * columns]
            return carry

        lax.fori_loop(0, rows, partial_row, 0)

    core = me % 2
    half = group * owned // 2
    grain = owned

    def invert(at, carry):
        place = at // owned
        high = place // (group // 2)
        odd = (high + me) % 2
        other = high
        for step in range(1, bits):
            bit = (place >> (bits - 1 - step)) & 1
            other = other | jnp.where(odd == 0, bit << step, bit << (bits - step))
        slot = (me ^ other) * owned + at % owned
        found = count
        for row in range(rows):
            for n in range(kp):
                for m in range(kp):
                    named = (row * kp + n) * kp + m
                    found = jnp.where(slots_ref[n, m, row] == slot, named, found)
        inverse[at] = found
        return carry

    def partner(step):
        def flip(bit):
            return me + bit * (1 - 2 * ((me // bit) % 2))

        if step == 0:
            return flip(1)
        return (1 - core) * flip(1 << step) + core * flip(1 << (bits - step))

    def half_copy(step, s, chunk):
        at = chunk * grain
        if step == 0:
            source = outgoing.at[s, pl.ds(at, grain)]
        else:
            source = total.at[s, pl.ds((half >> step) + at, grain)]
        return pltpu.make_async_remote_copy(
            src_ref=source,
            dst_ref=landed[step].at[s, pl.ds(at, grain)],
            send_sem=half_send_sem.at[step, s, chunk],
            recv_sem=half_recv_sem.at[step, s, chunk],
            device_id=(gx, partner(step)),
            device_id_type=MESH,
        )

    def send_partials(s):
        def send_chunk(turn, carry):
            chunk = half // grain - 1 - turn
            for j in range(grain):
                at = chunk * grain + j
                outgoing[s, at] = partial[s, inverse[half + at]]
            half_copy(0, s, chunk).start()
            return carry

        lax.fori_loop(0, half // grain, send_chunk, 0)

    def add_partials(step, s):
        last = step == bits - 1
        chunks = (half >> step) // grain

        def add(chunk):
            half_copy(step, s, chunk).wait_recv()
            for j in range(grain):
                at = chunk * grain + j
                mine = partial[s, inverse[at]] if step == 0 else total[s, at]
                value = mine.astype(jnp.float32) + landed[step][s, at].astype(jnp.float32)
                if last:
                    coarse_ref[at, :, s * columns : (s + 1) * columns] = value.astype(jnp.bfloat16)
                else:
                    total[s, at] = value.astype(jnp.bfloat16)

        if last:
            for chunk in reversed(range(chunks)):
                add(chunk)
            return

        def upper(turn, carry):
            chunk = chunks - 1 - turn
            add(chunk)
            half_copy(step + 1, s, chunk - chunks // 2).start()
            return carry

        def lower(turn, carry):
            add(chunks // 2 - 1 - turn)
            return carry

        lax.fori_loop(0, chunks // 2, upper, 0)
        lax.fori_loop(0, chunks // 2, lower, 0)

    stripes = range(STRIPES)
    load_peers.wait()
    load_slabs.wait()
    load_rows(0).wait()
    post_rows(0, 0)
    zero = jnp.zeros((width, columns), jnp.bfloat16)
    for s in range(STRIPES):
        owns[s][own_zero] = zero
        for rem in rems:
            rem[s][rem_zero] = zero
        partial[s, count] = zero
    load_matches.wait()
    load_locals.wait()
    load_remotes.wait()
    lax.fori_loop(0, rows, tabulate, 0)
    for s in stripes[1:]:
        load_rows(s).wait()
    load_operator.wait()
    for s in stripes:
        local_rows(s)
    for s in stripes[1:]:
        post_rows(0, s)
    load_slots.wait()
    lax.fori_loop(0, group * owned, invert, 0)
    load_diagonal.wait()

    stores = []
    for step in range(2):
        for s in stripes:
            arrive(step, s)
            smooth_rows(step, s)
            if s == STRIPES - 1:
                local_rows(s)
                if step == 1:
                    lax.fori_loop(0, rows, turn_row, 0)
            post_rows(step + 1, s)
            if step == 1:
                store = pltpu.make_async_copy(
                    owns[s].at[pl.ds(0, own_zero)],
                    smooth_hbm.at[:, :, pl.ds(s * columns, columns)],
                    out_sem.at[s],
                )
                store.start()
                stores.append(store)
            if s < STRIPES - 1:
                local_rows(s)

    for s in stripes:
        if s > 0:
            add_partials(0, s - 1)
        arrive(2, s)
        partial_rows(2, s)
        send_partials(s)
    for step in range(1, bits):
        add_partials(step, 0)
        add_partials(step - 1, 1)
    add_partials(bits - 1, 1)
    for s in stripes:
        for step in range(bits):
            for chunk in range((half >> step) // grain):
                half_copy(step, s, chunk).wait_send()
    for store in stores:
        store.wait()


def deliver(pieces, smooth_ref, coarse_ref, smooth_out, coarse_out, sem):
    copies = []
    for which, (source, target) in enumerate(((smooth_ref, smooth_out), (coarse_ref, coarse_out))):
        step = pl.cdiv(source.shape[0], pieces)
        for piece, at in enumerate(range(0, source.shape[0], step)):
            window = pl.ds(at, min(step, source.shape[0] - at))
            copies.append(
                pltpu.make_async_copy(
                    source.at[window], target.at[window], sem.at[which, piece]
                )
            )
    for copy in copies:
        copy.start()
    for copy in copies:
        copy.wait()


def body(
    operator_blocks,
    local_columns,
    remote_columns,
    match_slots,
    tentative,
    inverse_diagonal,
    peer_sends,
    slab_sends,
    coarse_slots,
):
    slabs = lax.axis_size("gx")
    group = lax.axis_size("gy")
    rows, kp, width = tentative.shape[:3]
    kl, ko = local_columns.shape[1], remote_columns.shape[1]
    peers = peer_sends.shape[1] // group
    halo = slab_sends.shape[1] // 2
    owned = (3 * rows * kp * kp // 2 + group - 1) // group
    bits = group.bit_length() - 1
    count = rows * kp * kp
    columns = width // STRIPES
    dims = (slabs, group, rows, kl, ko, kp, peers, halo, owned)

    def blocks(n):
        return pltpu.VMEM((STRIPES, n, width, columns), jnp.bfloat16)

    tables = (
        local_columns.T,
        remote_columns.T,
        match_slots.transpose(1, 2, 0),
        peer_sends,
        slab_sends,
        coarse_slots.transpose(1, 2, 0),
    )
    arrays = (operator_blocks, tentative.reshape(rows * kp, width, width), inverse_diagonal)
    anywhere = pl.BlockSpec(memory_space=pl.ANY)
    half = group * owned // 2
    remote_count = (group * peers + 2 * halo) * kp
    vmem = [
        pltpu.VMEM(operator_blocks.shape, jnp.bfloat16),
        pltpu.VMEM((rows, width, width), jnp.bfloat16),
        blocks(remote_count),
        pltpu.VMEM((STRIPES, rows, width, kp * columns), jnp.float32),
        pltpu.VMEM((rows, kp * width, width), jnp.bfloat16),
        blocks(count + 1),
        blocks(half),
        blocks(half),
    ]
    striped = [pltpu.VMEM((rows * kp + 1, width, columns), jnp.bfloat16)] * STRIPES
    striped += [pltpu.VMEM((remote_count + 1, width, columns), jnp.bfloat16)] * (2 * STRIPES)
    landed = [blocks(half >> step) for step in range(bits)]
    used = sum(
        math.prod(x.shape) * jnp.dtype(x.dtype).itemsize for x in [*vmem, *striped, *landed]
    )
    grant = used + owned * width * width * 2 + (1 << 20)
    smoothed, coarse = pl.pallas_call(
        functools.partial(kernel, dims),
        out_shape=(
            jax.ShapeDtypeStruct((rows * kp, width, width), jnp.bfloat16),
            jax.ShapeDtypeStruct((owned, width, width), jnp.bfloat16),
        ),
        in_specs=[pl.BlockSpec(memory_space=pltpu.HBM)] * 9,
        out_specs=(anywhere, pl.BlockSpec(memory_space=pltpu.VMEM)),
        scratch_shapes=[
            *vmem,
            *[pltpu.SMEM(table.shape, jnp.int32) for table in tables],
            pltpu.SMEM((kl + ko, kp, rows), jnp.int32),
            pltpu.SMEM((2 * half,), jnp.int32),
            *striped,
            *landed,
            pltpu.SemaphoreType.DMA((len(tables),)),
            pltpu.SemaphoreType.DMA((2,)),
            pltpu.SemaphoreType.DMA((STRIPES,)),
            pltpu.SemaphoreType.DMA((STRIPES,)),
            pltpu.SemaphoreType.DMA((3, STRIPES, group)),
            pltpu.SemaphoreType.DMA((3, STRIPES, group)),
            pltpu.SemaphoreType.DMA((3, STRIPES, 2)),
            pltpu.SemaphoreType.DMA((3, STRIPES, 2)),
            pltpu.SemaphoreType.DMA((bits, STRIPES, group)),
            pltpu.SemaphoreType.DMA((bits, STRIPES, group)),
        ],
        compiler_params=pltpu.CompilerParams(
            collective_id=0, has_side_effects=True, vmem_limit_bytes=grant
        ),
    )(*[pltpu.with_memory_space_constraint(x, pltpu.HBM) for x in tables + arrays])
    pieces = 1
    results = [pltpu.with_memory_space_constraint(x, pltpu.VMEM) for x in (smoothed, coarse)]
    smoothed, coarse = pl.pallas_call(
        functools.partial(deliver, pieces),
        out_shape=tuple(jax.ShapeDtypeStruct(x.shape, x.dtype) for x in (smoothed, coarse)),
        in_specs=[pl.BlockSpec(memory_space=pltpu.VMEM)] * 2,
        out_specs=(anywhere, anywhere),
        scratch_shapes=[pltpu.SemaphoreType.DMA((2, pieces))],
    )(*results)
    return smoothed.reshape(tentative.shape), coarse


def solution(mesh):
    placed = (
        P(("gx", "gy"), None, None, None),
        P(("gx", "gy"), None),
        P(("gx", "gy"), None),
        P(("gx", "gy"), None, None),
        P(("gx", "gy"), None, None, None),
        P(("gx", "gy"), None, None),
        P(("gx", "gy"), None),
        P(("gx", "gy"), None),
        P(("gx", "gy"), None, None),
    )
    return jax.shard_map(
        body,
        mesh=mesh,
        in_specs=placed,
        out_specs=(P(("gx", "gy"), None, None, None), P(("gx", "gy"), None, None)),
        check_vma=False,
    )
```
